128 devices in a mesh: gx: 4 (over z), gy: 4 (over y), gz: 8 (over x, core).
Axes of the slice: x: 4, y: 4, z: 4, core: 2. Of those that a mesh axis runs over, the one named last changes fastest.
Arguments:
- features: bfloat16 [32768, 1024], P(('gx', 'gy', 'gz')), may hold values from -6 to 6
- cotangent: bfloat16 [32768, 1024], P(('gx', 'gy', 'gz')), may hold values from -6 to 6
- leaf_device: int32 [32768, 1], P(('gx', 'gy', 'gz')), may hold values from 0 to 127; in each aligned block of 256 rows (0 to 255, 256 to 511, ...) at most 4 rows name the same one
- neighbours: int32 [16, 65536], P(None, ('gx', 'gy', 'gz')), may hold values from 0 to 511
- radial: float32 [64, 65536], P(None, ('gx', 'gy', 'gz')), may hold values from 0.25 to 2
- first_zero: bfloat16 [256, 256], replicated, may hold values from -0.375 to 0.375
- first_one: bfloat16 [192, 192], replicated, may hold values from -0.4375 to 0.4375
- first_two: bfloat16 [128, 128], replicated, may hold values from -0.5 to 0.5
- first_three: bfloat16 [64, 64], replicated, may hold values from -0.75 to 0.75
- second_zero: bfloat16 [256, 256], replicated, may hold values from -0.375 to 0.375
- second_one: bfloat16 [192, 192], replicated, may hold values from -0.4375 to 0.4375
- second_two: bfloat16 [128, 128], replicated, may hold values from -0.5 to 0.5
- second_three: bfloat16 [64, 64], replicated, may hold values from -0.75 to 0.75
- lift_leaf: float32 [8, 16, 16], replicated, may hold values from -0.5 to 0.5
- lift_branch: float32 [4, 16, 16], replicated, may hold values from -0.75 to 0.75
- couple_root: float32 [4, 4, 16, 16], replicated, may hold values from -0.75 to 0.75
- couple_branch: float32 [4, 4, 16, 16], replicated, may hold values from -0.75 to 0.75
- couple_leaf: float32 [8, 8, 16, 16], replicated, may hold values from -0.5 to 0.5
Outputs:
- updated: bfloat16 [32768, 1024], P(('gx', 'gy', 'gz'))
- radial_grad: float32 [64, 65536], P(None, ('gx', 'gy', 'gz'))
The draws below stay inside these ranges and needn't reach their ends.
Inputs may be any that keep to these rules, and one draw needn't show every extreme that they name: `leaf_device`: among the 256 atoms of one brick at most 4 have the same leaf; every leaf holds at least one atom.
All inputs are finite; a program needn't handle non-finite values.
Results may differ from the reference program's by a relative error of at most 0.0037.
Values may be sent and summed in bfloat16 or wider, within the bound.
No kernel may reach another device: no remote copies, remote signals or barrier semaphores. Data moves between devices by JAX's collectives and lax.ppermute only.
A program may use at most 64 MiB of HBM per device.

```python
import math
import jax
import jax.numpy as jnp
import numpy as np
from jax import lax

C = 64
F = 1024
NBR = 16
A_DEV = 256
ATOMS = 32768
CAP = 4
POOL = 512
POOLS = 65536
N_GX = 4
N_GY = 4
N_GZ = 8
DEVICES = 128


def touch_ends(values, own_key, smallest, largest):
    spot = [jax.random.randint(jax.random.fold_in(own_key, axis), (), 0, length) for axis, length in enumerate(values.shape)]
    main_axis = values.shape.index(max(values.shape))
    next_to = spot[:main_axis] + [(spot[main_axis] + 1) % values.shape[main_axis]] + spot[main_axis + 1:]
    return values.at[tuple(spot)].set(smallest).at[tuple(next_to)].set(largest)


def level_of(rng, dims, cuts, least, largest):
    gain, own = 1.0, jax.random.fold_in(rng, 6)
    for position, blocks in cuts:
        steps = jnp.exp(jax.random.uniform(jax.random.fold_in(own, position), (blocks,), jnp.float32, least / len(cuts), largest / len(cuts)))
        gain = gain * jnp.repeat(steps, dims[position] // blocks).reshape([-1 if axis == position else 1 for axis in range(len(dims))])
    return gain


def deal_out(key, own, number, rows, number_of, top, most, slope):
    sequence = jax.random.permutation(key, number_of)
    crowded, common = load_shares(number_of, rows * top, most, slope, True), load_shares(number_of, rows * top, most, slope, False)
    places = jnp.arange(number_of)

    def named(tallies, rotation):
        used = int((tallies > 0).sum())
        fixed = max(1, used // 4)
        passed = fixed + (places - fixed + rotation * (used - fixed)) % max(1, number_of - fixed)
        return jnp.zeros((number_of,), jnp.int32).at[sequence[jnp.where(places < fixed, places, passed)]].set(jnp.asarray(tallies, jnp.int32))

    tallies = jnp.where(number % 4 == 0, named(crowded, number // 4), named(common, number - number // 4 - 1))
    mixed = jax.random.permutation(jax.random.fold_in(own, 3), number_of)
    donor, taker = mixed[0:number_of // 2 * 2:2], mixed[1:number_of // 2 * 2:2]
    margin = jnp.minimum(tallies[donor] - 1, most - tallies[taker]) // 2
    margin = jnp.where((donor == sequence[0]) | (taker == sequence[0]) | (tallies[taker] == 0), 0, jnp.maximum(margin, 0))
    passed = jax.random.randint(jax.random.fold_in(own, 4), (number_of // 2,), 0, 1 << 20) % (margin + 1)
    tallies = tallies.at[donor].add(-passed).at[taker].add(passed)
    members = jnp.searchsorted(jnp.cumsum(tallies), jnp.arange(rows * top), side="right").astype(jnp.int32)
    table = members.reshape(top, rows).T
    table = table[jax.random.permutation(jax.random.fold_in(own, 1), rows)]
    rotation = jax.random.randint(jax.random.fold_in(own, 2), (rows, 1), 0, top)
    return jnp.take_along_axis(table, (jnp.arange(top)[None, :] + rotation) % top, axis=1)


def load_shares(count, total, bound, lean, full):
    loads = [(1 << 20) // math.isqrt(grade ** lean) + 1 for grade in range(1, count + 1)]
    largest = bound if full else min(bound, max(-(-total // count), total * loads[0] // sum(loads)))
    least = 1 if total - largest >= count - 1 else 0
    counts, rest = [largest] + [least] * (count - 1), total - largest - least * (count - 1)
    while rest > 0:
        movable = [i for i in range(1, count) if counts[i] < largest] or [i for i in range(1, count) if counts[i] < bound]
        pool, budget = sum([loads[i] for i in movable]), rest
        for i in movable:
            extra = min(bound - counts[i], max(1, budget * loads[i] // pool), rest)
            counts[i] = counts[i] + extra
            rest = rest - extra
    return np.array(counts)


def centred(rng, dims, scale, bound, cuts=(), held_as=jnp.bfloat16):
    loudness = level_of(rng, dims, cuts, -0.22, 0.18) if cuts else 1.0
    values = jax.random.normal(rng, dims, jnp.float32) * scale * loudness
    return jnp.minimum(jnp.maximum(values, -bound), bound).astype(held_as)


def setup_inputs(seed: int = 0) -> dict:
    arg_keys = jax.random.split(jax.random.key(seed), 19)
    features = centred(arg_keys[0], (ATOMS, F), 1.0, 6.0, ((0, 128),))
    cotangent = centred(arg_keys[1], (ATOMS, F), 1.0, 6.0, ((0, 128),))
    leaf_device_keys = jax.random.split(jax.random.fold_in(arg_keys[2], 1), ATOMS // A_DEV)
    leaf_device_turns = jax.random.permutation(jax.random.fold_in(arg_keys[2], 3), ATOMS // A_DEV)
    leaf_device = jax.vmap(lambda own, number: deal_out(jax.random.fold_in(arg_keys[2], 2), own, number, A_DEV, DEVICES, 1, CAP, 2))(leaf_device_keys, leaf_device_turns).reshape((ATOMS, 1))
    neighbours = touch_ends(jax.random.randint(arg_keys[3], (NBR, POOLS), 0, POOL), jax.random.fold_in(arg_keys[3], 1), 0, POOL - 1).astype(jnp.int32)
    radial = jnp.clip(jnp.exp(math.log(2.0) - 2.0794415 * jax.random.uniform(arg_keys[4], (NBR * 4, POOLS), jnp.float32) ** level_of(arg_keys[4], (NBR * 4, POOLS), ((1, 128),), -0.2, 0.2)), 0.25, 2.0)
    first_zero = centred(arg_keys[5], (4 * C, 4 * C), (4 * C) ** -0.5, 0.375)
    first_one = centred(arg_keys[6], (3 * C, 3 * C), (3 * C) ** -0.5, 0.4375)
    first_two = centred(arg_keys[7], (2 * C, 2 * C), (2 * C) ** -0.5, 0.5)
    first_three = centred(arg_keys[8], (C, C), C ** -0.5, 0.75)
    second_zero = centred(arg_keys[9], (4 * C, 4 * C), (4 * C) ** -0.5, 0.375)
    second_one = centred(arg_keys[10], (3 * C, 3 * C), (3 * C) ** -0.5, 0.4375)
    second_two = centred(arg_keys[11], (2 * C, 2 * C), (2 * C) ** -0.5, 0.5)
    second_three = centred(arg_keys[12], (C, C), C ** -0.5, 0.75)
    lift_leaf = centred(arg_keys[13], (N_GZ, 16, 16), (16 * N_GZ) ** -0.5, 0.5, (), jnp.float32)
    lift_branch = centred(arg_keys[14], (N_GY, 16, 16), (16 * N_GY) ** -0.5, 0.75, (), jnp.float32)
    couple_root = centred(arg_keys[15], (N_GX, N_GX, 16, 16), (16 * N_GX) ** -0.5, 0.75, (), jnp.float32)
    couple_branch = centred(arg_keys[16], (N_GY, N_GY, 16, 16), (16 * N_GY) ** -0.5, 0.75, (), jnp.float32)
    couple_leaf = centred(arg_keys[17], (N_GZ, N_GZ, 16, 16), (16 * N_GZ) ** -0.5, 0.5, (), jnp.float32)
    return dict(features=features, cotangent=cotangent, leaf_device=leaf_device, neighbours=neighbours, radial=radial, first_zero=first_zero, first_one=first_one, first_two=first_two, first_three=first_three, second_zero=second_zero, second_one=second_one, second_two=second_two, second_three=second_three, lift_leaf=lift_leaf, lift_branch=lift_branch, couple_root=couple_root, couple_branch=couple_branch, couple_leaf=couple_leaf)


DEGREES = (0, 1, 2, 3, 1, 2, 3, 1, 2, 3, 2, 3, 2, 3, 3, 3)

def mix_ref(values, mats, flip):
    chans = mats[3].shape[0]
    count = values.shape[0]
    form = 'rsk,jk->rsj' if flip else 'rsk,kj->rsj'
    pieces = [values[:, :4 * chans].reshape(count, 1, 4 * chans), values[:, 4 * chans:10 * chans].reshape(count, 2, 3 * chans), values[:, 10 * chans:14 * chans].reshape(count, 2, 2 * chans), values[:, 14 * chans:].reshape(count, 2, chans)]
    outs = []
    for piece, weight in zip(pieces, mats):
        result = jnp.einsum(form, piece.astype(jnp.float32), weight.astype(jnp.float32))
        outs.append(result.reshape(count, -1))
    return jnp.concatenate(outs, axis=1)

def leaf_work(pool_feat, pool_grad, nbrs, rads, local3, occ_int, firsts, seconds):
    count, width = pool_feat.shape
    chans = width // 16
    select = jnp.asarray(np.eye(4, dtype=np.float32)[list(DEGREES)])
    trans = mix_ref(pool_grad, seconds, True)
    order = jnp.argsort(1 - occ_int, stable=True).astype(jnp.int32)
    filled = jnp.sum(occ_int).astype(jnp.int32)
    occ = occ_int.astype(jnp.float32)

    def step(carry, item):
        choose, rad4 = item
        index = order[(choose % filled).astype(jnp.int32)]
        other = pool_feat[index]
        summed = pool_feat.astype(jnp.float32) + other.astype(jnp.float32)
        scales = rad4[np.array(DEGREES)].T
        zeta = (summed.reshape(count, 16, chans) * scales[:, :, None]).reshape(count, width).astype(jnp.bfloat16)
        upper = mix_ref(zeta, firsts, False)
        value = jax.nn.silu(upper).astype(jnp.bfloat16)
        message = mix_ref(value, seconds, False)
        sig = jax.nn.sigmoid(upper)
        grad_u = (sig * (1.0 + upper * (1.0 - sig)) * trans).astype(jnp.bfloat16)
        back = mix_ref(grad_u, firsts, True)
        per_coef = lax.optimization_barrier(jnp.sum((back * summed).reshape(count, 16, chans), axis=2))
        dradial = 0.25 * occ[:, None] * jnp.dot(per_coef, select, precision=lax.Precision.HIGHEST)
        return (carry + message, dradial.T)
    near, dr = lax.scan(step, jnp.zeros((count, width), jnp.float32), (nbrs, rads.reshape(-1, 4, count)))
    near = 0.25 * occ[:, None] * near
    feat = pool_feat.astype(jnp.float32)
    out = (feat + near + feat * local3.reshape(1, width)).astype(jnp.bfloat16)
    return (out, dr.reshape(-1, count))

def reference(features, cotangent, leaf_device, neighbours, radial, first_zero, first_one, first_two, first_three, second_zero, second_one, second_two, second_three, lift_leaf, lift_branch, couple_root, couple_branch, couple_leaf):
    hp = lax.Precision.HIGHEST
    target = leaf_device[:, 0].reshape(DEVICES, A_DEV)
    onehot = (target[:, :, None] == jnp.arange(DEVICES, dtype=jnp.int32)[None, None, :]).astype(jnp.int32)
    rank = lax.optimization_barrier(jnp.sum(jnp.cumsum(onehot, axis=1) * onehot, axis=2)) - 1
    source = jnp.arange(DEVICES, dtype=jnp.int32)[:, None]
    slot = (target * POOL + source * CAP + rank).reshape(ATOMS).astype(jnp.int32)
    occupied = jnp.zeros((DEVICES * POOL,), jnp.int32).at[slot].set(1).reshape(DEVICES, POOL)
    pool_feat = jnp.zeros((DEVICES * POOL, F), jnp.bfloat16).at[slot].set(features).reshape(DEVICES, POOL, F)
    pool_grad = jnp.zeros((DEVICES * POOL, F), jnp.bfloat16).at[slot].set(cotangent).reshape(DEVICES, POOL, F)
    leaf = (lax.optimization_barrier(jnp.sum(pool_feat, axis=1, dtype=jnp.float32)) / math.sqrt(A_DEV)).reshape(N_GX, N_GY, N_GZ, 16, C)
    mids = jnp.einsum('kpq,abkqc->abpc', lift_leaf, leaf, precision=hp)
    tops = jnp.einsum('bpq,abqc->apc', lift_branch, mids, precision=hp)
    root_mask = couple_root * (1.0 - jnp.eye(N_GX, dtype=jnp.float32))[:, :, None, None]
    branch_mask = couple_branch * (1.0 - jnp.eye(N_GY, dtype=jnp.float32))[:, :, None, None]
    leaf_mask = couple_leaf * (1.0 - jnp.eye(N_GZ, dtype=jnp.float32))[:, :, None, None]
    local1 = jnp.einsum('ajpq,jqc->apc', root_mask, tops, precision=hp)
    local2 = jnp.einsum('bqp,aqc->abpc', lift_branch, local1, precision=hp) + jnp.einsum('bjpq,ajqc->abpc', branch_mask, mids, precision=hp)
    local3 = jnp.einsum('kqp,abqc->abkpc', lift_leaf, local2, precision=hp) + jnp.einsum('kjpq,abjqc->abkpc', leaf_mask, leaf, precision=hp)
    local3 = local3.reshape(DEVICES, 16, C)
    nbr_dev = neighbours.reshape(NBR, DEVICES, POOL).transpose(1, 0, 2)
    rad_dev = radial.reshape(NBR * 4, DEVICES, POOL).transpose(1, 0, 2)
    firsts = (first_zero, first_one, first_two, first_three)
    seconds = (second_zero, second_one, second_two, second_three)

    def per_leaf(item):
        return leaf_work(item[0], item[1], item[2], item[3], item[4], item[5], firsts, seconds)
    pool_out, dr = lax.map(per_leaf, (pool_feat, pool_grad, nbr_dev, rad_dev, local3, occupied))
    updated = pool_out.reshape(DEVICES * POOL, F)[slot]
    radial_grad = dr.transpose(1, 0, 2).reshape(NBR * 4, POOLS)
    return (updated, radial_grad)
```

```python
import math

import jax
import jax.numpy as jnp
import numpy as np
from jax import lax
from jax.experimental import pallas as pl
from jax.experimental.pallas import tpu as pltpu
from jax.sharding import PartitionSpec as P

BF16 = jnp.bfloat16
F32 = jnp.float32
HIGHEST = lax.Precision.HIGHEST
AXES = ("gx", "gy", "gz")
EMPTY = 1024.0
ROWS = 256
POOL = 512
WIDTH = 1024
NBR = 16
TILE = 256


def dot(a, b, **kw):
    return jnp.dot(a, b, preferred_element_type=F32, **kw)


def iota(shape, axis):
    return lax.broadcasted_iota(jnp.int32, shape, axis)


def row_of(col):
    n = col.shape[0]
    diag = jnp.where(iota((n, n), 0) == iota((n, n), 1), col.astype(F32), 0.0).astype(BF16)
    return dot(jnp.ones((8, n), BF16), diag)[0:1, :].astype(jnp.int32)


def pack_kernel(leaf_ref, feat_ref, grad_ref, send_ref):
    col = leaf_ref[...]
    row = row_of(col)
    n = ROWS
    same = (col == row) & (iota((n, n), 0) < iota((n, n), 1))
    rank = jnp.sum(jnp.where(same, 1.0, 0.0), axis=0, keepdims=True).astype(jnp.int32)
    slot = row * 8 + rank
    ones = jnp.ones((n, 128), BF16)
    for part in range(4):
        index = iota((n, n), 0) + part * n
        pick_f = jnp.where(index == slot, 1.0, 0.0).astype(BF16)
        pick_g = jnp.where(index == slot + 4, 1.0, 0.0).astype(BF16)
        there = dot(pick_f, ones)
        gone = (there < 0.5) & ((iota((n, 128), 0) & 7) < 4)
        out = dot(pick_f, feat_ref[...]) + dot(pick_g, grad_ref[...])
        send_ref[part * n : (part + 1) * n, 128:] = out[:, 128:].astype(BF16)
        send_ref[part * n : (part + 1) * n, :128] = jnp.where(gone, EMPTY, out[:, :128]).astype(BF16)


def pack(leaf_device, features, cotangent):
    return pl.pallas_call(
        pack_kernel,
        out_shape=jax.ShapeDtypeStruct((128 * 8, WIDTH), BF16),
        name="pack",
    )(leaf_device, features, cotangent)


def mix(x, w0, w1a, w1b, w2, w3):
    a = dot(x[:, 0:256], w0)
    b = dot(x[:, 256:512], w1a)
    c = dot(x[:, 384:640], w1b)
    d = dot(x[:, 640:896], w2)
    e = dot(x[:, 896:1024], w3)
    return [
        a[:, :128],
        a[:, 128:],
        b[:, :128],
        b[:, 128:] + c[:, :128],
        c[:, 128:],
        d[:, :128],
        d[:, 128:],
        e,
    ]


def gather_rows(perm_ref, m_ref, fc_ref, rows, k):
    size = rows.size
    shifted = pltpu.roll(m_ref[rows, :], (128 - k) % 128, 1)
    pick = jnp.broadcast_to(shifted[:, 0:1], (size, POOL))
    own = perm_ref[rows, :]
    hot = jnp.where(iota((size, POOL), 1).astype(F32) == pick, own + 1.0, own)
    return dot(hot.astype(BF16), fc_ref[...])


def scales(rad_ref, rows, k):
    size = rows.size
    shifted = pltpu.roll(rad_ref[rows, :], (128 - 4 * k) % 128, 1)
    r0, r1, r2, r3 = [jnp.broadcast_to(shifted[:, j : j + 1], (size, 128)) for j in range(4)]
    low = iota((size, 128), 1) < 64
    p01 = jnp.where(low, r0, r1)
    p23 = jnp.where(low, r2, r3)
    p12 = jnp.where(low, r1, r2)
    p31 = jnp.where(low, r3, r1)
    return [p01, p23, p12, p31, p23, p23, p23, r3]


def leaf_a_kernel(
    got_ref,
    nbr_ref,
    rad_ref,
    f0, f1a, f1b, f2, f3,
    s0, s1a, s1b, s2, s3,
    t0, t1a, t1b, t2, t3,
    gu_ref,
    back_ref,
    fc_ref,
    perm_ref,
    m_ref,
    acc_ref,
    half_t_ref,
):
    k = pl.program_id(0)

    @pl.when(k == 0)
    def _():
        first = jnp.where(iota((8, 128), 1) == 0, 1.0, 0.0).astype(BF16)
        got0 = got_ref[:, :, :, 0:128].reshape(1024, 128)
        lead = lax.dot_general(first, got0, (((1,), (1,)), ((), ())), preferred_element_type=F32)
        lane = iota((8, 1024), 1)
        occ = jnp.where((lead < 0.5 * EMPTY) & ((lane & 7) < 4), 1.0, 0.0)
        filled = jnp.sum(occ[0:1, :], axis=1, keepdims=True)
        before = jnp.where(iota((1024, 1024), 0) < iota((1024, 1024), 1), 1.0, 0.0).astype(BF16)
        rank = dot(occ.astype(BF16), before)
        rank = jnp.where(occ > 0.5, rank, -1.0)
        compact = jnp.where(iota((POOL, 1024), 0).astype(F32) == rank[0:1, :], 1.0, 0.0).astype(BF16)
        got = got_ref[...].reshape(1024, WIDTH)
        fc_ref[...] = dot(compact, got).astype(BF16)
        slot = iota((POOL, 1024), 0)
        where_from = (slot >> 2) * 8 + (slot & 3)
        pick = jnp.where(iota((POOL, 1024), 1) == where_from, 1.0, 0.0).astype(BF16)
        perm_ref[...] = lax.dot_general(
            pick, compact, (((1,), (1,)), ((), ())), preferred_element_type=F32
        )
        pick_t = jnp.where(iota((POOL, 1024), 1) == where_from + 4, 1.0, 0.0).astype(BF16)
        grad = dot(pick_t, got).astype(BF16)
        mixed = mix(grad, t0[...], t1a[...], t1b[...], t2[...], t3[...])
        half_t_ref[...] = 0.5 * jnp.concatenate(mixed, axis=1)
        choice = nbr_ref[...].astype(F32)
        turns = jnp.floor(choice / filled)
        left = choice - turns * filled
        left = jnp.where(left < 0.0, left + filled, left)
        m_ref[...] = jnp.where(left >= filled, left - filled, left)
        acc_ref[...] = jnp.zeros_like(acc_ref)

    for part in range(POOL // TILE):
        rows = pl.ds(part * TILE, TILE)
        y = gather_rows(perm_ref, m_ref, fc_ref, rows, k)
        pats = scales(rad_ref, rows, k)
        z = jnp.concatenate([(y[:, g * 128 : (g + 1) * 128] * pats[g]).astype(BF16) for g in range(8)], axis=1)
        w = mix(z, f0[...], f1a[...], f1b[...], f2[...], f3[...])
        for g in range(8):
            cols = slice(g * 128, (g + 1) * 128)
            h = jnp.tanh(w[g])
            up = 1.0 + h
            v = w[g] * up
            acc_ref[rows, cols] += v
            gu_ref[0, rows, cols] = ((up + v * (1.0 - h)) * half_t_ref[rows, cols]).astype(BF16)

    @pl.when(k == NBR - 1)
    def _():
        total = acc_ref[...]
        high = total.astype(BF16)
        low = (total - high.astype(F32)).astype(BF16)
        wts = (s0[...], s1a[...], s1b[...], s2[...], s3[...])
        near = [0.25 * (a + b) for a, b in zip(mix(high, *wts), mix(low, *wts))]
        half = iota((64, 8, 512), 1) < 4
        lo = jnp.concatenate(near[:4], axis=1)
        hi = jnp.concatenate(near[4:], axis=1)
        lo_r = pltpu.roll(lo.reshape(64, 8, 512), 4, 1)
        hi_r = pltpu.roll(hi.reshape(64, 8, 512), 4, 1)
        lo = lo.reshape(64, 8, 512)
        hi = hi.reshape(64, 8, 512)
        back_ref[:, 0, :, :512] = jnp.where(half, lo, hi_r).astype(BF16)
        back_ref[:, 1, :, :512] = jnp.where(half, lo_r, hi).astype(BF16)
        tile = jnp.sum(fc_ref[...].astype(F32), axis=0, keepdims=True) / math.sqrt(ROWS)
        body = jnp.concatenate([tile[:, r * 128 : (r + 1) * 128] for r in range(8)], axis=0)
        body = jnp.broadcast_to(body[None, None], (64, 2, 8, 128)).astype(BF16)
        back_ref[:, :, :, 512:] = body


def leaf_a(got, nbr, rad, firsts, seconds, trans):
    full = lambda x: pl.BlockSpec(x.shape, lambda k, n=len(x.shape): (0,) * n)
    args = (got, nbr, rad, *firsts, *seconds, *trans)
    return pl.pallas_call(
        leaf_a_kernel,
        grid=(NBR,),
        in_specs=[full(x) for x in args],
        out_specs=[
            pl.BlockSpec((1, POOL, WIDTH), lambda k: (k, 0, 0)),
            pl.BlockSpec((64, 2, 8, 640), lambda k: (0, 0, 0, 0)),
            pl.BlockSpec((POOL, WIDTH), lambda k: (0, 0)),
            pl.BlockSpec((POOL, POOL), lambda k: (0, 0)),
            pl.BlockSpec((POOL, 128), lambda k: (0, 0)),
        ],
        out_shape=[
            jax.ShapeDtypeStruct((NBR, POOL, WIDTH), BF16),
            jax.ShapeDtypeStruct((64, 2, 8, 640), BF16),
            jax.ShapeDtypeStruct((POOL, WIDTH), BF16),
            jax.ShapeDtypeStruct((POOL, POOL), F32),
            jax.ShapeDtypeStruct((POOL, 128), F32),
        ],
        scratch_shapes=[pltpu.VMEM((POOL, WIDTH), F32), pltpu.VMEM((POOL, WIDTH), F32)],
        compiler_params=pltpu.CompilerParams(vmem_limit_bytes=56 << 20),
        cost_estimate=pl.CostEstimate(flops=12 << 30, bytes_accessed=24 << 20, transcendentals=8 << 20),
        name="leaf_a",
    )(*args)


PATTERN = ((0, 1), (2, 3), (1, 2), (3, 1), (3, 3))


def leaf_b_kernel(gu_ref, fc_ref, perm_ref, m_ref, t0, t1a, t1b, t2, t3, table_ref, out_ref, acc_ref):
    k = pl.program_id(0)

    @pl.when(k == 0)
    def _():
        acc_ref[...] = jnp.zeros_like(acc_ref)

    for part in range(POOL // TILE):
        rows = pl.ds(part * TILE, TILE)
        y = gather_rows(perm_ref, m_ref, fc_ref, rows, k)
        s = mix(gu_ref[0, rows, :], t0[...], t1a[...], t1b[...], t2[...], t3[...])
        p = [s[g] * y[:, g * 128 : (g + 1) * 128] for g in range(8)]
        q = jnp.concatenate([p[0], (p[1] + p[4]) + (p[5] + p[6]), p[2], p[3], p[7]], axis=1)
        high = q.astype(BF16)
        low = (q - high.astype(F32)).astype(BF16)
        sums = dot(high, table_ref[...]) + dot(low, table_ref[...])
        mine = (iota((TILE, 128), 1) >> 2) == k
        acc_ref[rows, :] += jnp.where(mine, sums, 0.0)

    @pl.when(k == NBR - 1)
    def _():
        occ = dot(perm_ref[...].astype(BF16), jnp.ones((POOL, 128), BF16))
        out_ref[...] = jnp.transpose(0.5 * occ * acc_ref[...])[0:64, :]


def leaf_b(gu, fc, perm, m, trans, table):
    full = lambda x: pl.BlockSpec(x.shape, lambda k, n=len(x.shape): (0,) * n)
    args = (fc, perm, m, *trans, table)
    return pl.pallas_call(
        leaf_b_kernel,
        grid=(NBR,),
        in_specs=[pl.BlockSpec((1, POOL, WIDTH), lambda k: (k, 0, 0))] + [full(x) for x in args],
        out_specs=pl.BlockSpec((64, POOL), lambda k: (0, 0)),
        out_shape=jax.ShapeDtypeStruct((64, POOL), F32),
        scratch_shapes=[pltpu.VMEM((POOL, 128), F32)],
        compiler_params=pltpu.CompilerParams(vmem_limit_bytes=40 << 20),
        cost_estimate=pl.CostEstimate(flops=12 << 30, bytes_accessed=24 << 20, transcendentals=0),
        name="leaf_b",
    )(gu, *args)


def block_swap(tiles):
    low = iota((8, 128), 1) < 64
    out = [[None] * 8 for _ in range(16)]
    for pair in range(8):
        for g in range(8):
            a, b = tiles[2 * pair][g], tiles[2 * pair + 1][g]
            out[2 * g][pair] = jnp.where(low, a, pltpu.roll(b, 64, 1))
            out[2 * g + 1][pair] = jnp.where(low, pltpu.roll(a, 64, 1), b)
    return out


def own_block(x):
    which = (iota((16, 1024), 1) >> 6) & 3
    out = x[0:16]
    for b in range(1, 4):
        out = jnp.where(which == b, x[b * 16 : (b + 1) * 16], out)
    return out


def finish_kernel(ret_ref, feat_ref, leaf_ref, up2_ref, up1_ref, root_ref, mid_ref, low_ref, out_ref, tile_ref):
    tile_ref[...] = ret_ref[:, 512:640].astype(F32)
    tiles = [[tile_ref[pl.ds(ab * 64 + g, 8, stride=8), :] for g in range(8)] for ab in range(16)]
    swapped = block_swap(tiles)
    s2 = jnp.concatenate([jnp.concatenate(row, axis=1) for row in swapped], axis=0)
    m2 = dot(up2_ref[...], s2, precision=HIGHEST)
    v = own_block(dot(up1_ref[...], m2, precision=HIGHEST))
    parts = []
    for a in range(4):
        s = v[:, a * 256 : a * 256 + 128] + v[:, a * 256 + 128 : a * 256 + 256]
        s = s + pltpu.roll(s, 64, 1)
        parts.append(jnp.concatenate([s, s], axis=1))
    m1 = jnp.concatenate(parts, axis=0)
    l1 = dot(root_ref[...], m1, precision=HIGHEST)
    l1 = jnp.concatenate([l1[a * 16 : (a + 1) * 16] for a in range(4)], axis=1)
    stack = [l1]
    for shift in range(1, 4):
        stack.append(
            jnp.concatenate(
                [pltpu.roll(m2[:, a * 256 : (a + 1) * 256], 256 - 64 * shift, 1) for a in range(4)], axis=1
            )
        )
    l2 = own_block(dot(mid_ref[...], jnp.concatenate(stack, axis=0), precision=HIGHEST))
    l3 = dot(low_ref[:, :128], s2, precision=HIGHEST) + dot(low_ref[:, 128:144], l2, precision=HIGHEST)
    swapped = block_swap([[l3[q * 8 : (q + 1) * 8, g * 128 : (g + 1) * 128] for g in range(8)] for q in range(16)])
    l3 = jnp.concatenate([jnp.concatenate(row, axis=1) for row in swapped], axis=0)
    l3_high = l3.astype(BF16)
    l3_low = (l3 - l3_high.astype(F32)).astype(BF16)

    n = ROWS
    col = leaf_ref[...]
    row = row_of(col)
    same = jnp.where((col == row) & (iota((n, n), 1) < iota((n, n), 0)), 1.0, 0.0).astype(BF16)
    rank = dot(same, jnp.ones((n, 128), BF16))[:, 0:1].astype(jnp.int32)
    slot = col * 8 + rank
    lane = iota((n, 1024), 1)
    near_lo = dot(jnp.where(lane == slot, 1.0, 0.0).astype(BF16), ret_ref[:, :512])
    near_hi = dot(jnp.where(lane == slot + 4, 1.0, 0.0).astype(BF16), ret_ref[:, :512])
    mine = jnp.where(iota((n, 128), 1) == col, 1.0, 0.0).astype(BF16)
    local = dot(mine, l3_high) + dot(mine, l3_low)
    feat = feat_ref[...].astype(F32)
    near = jnp.concatenate([near_lo, near_hi], axis=1)
    out_ref[...] = (feat + near + feat * local).astype(BF16)


def finish(ret, features, leaf_device, mats):
    return pl.pallas_call(
        finish_kernel,
        out_shape=jax.ShapeDtypeStruct((ROWS, WIDTH), BF16),
        scratch_shapes=[pltpu.VMEM((1024, 128), F32)],
        name="finish",
    )(ret, features, leaf_device, *mats)


def blocks(mats, scale, flip):
    m0, m1, m2, m3 = [(m.T if flip else m) * jnp.asarray(scale, m.dtype) for m in mats]
    w1a = jnp.pad(m1, ((0, 64), (0, 64)))
    w1b = jnp.pad(m1, ((64, 0), (64, 0)))
    w2 = jnp.pad(m2, ((0, 128), (0, 128))) + jnp.pad(m2, ((128, 0), (128, 0)))
    w3 = jnp.pad(m3, ((0, 64), (0, 64))) + jnp.pad(m3, ((64, 0), (64, 0)))
    return m0, w1a, w1b, w2, w3


def tree_mats(lift_leaf, lift_branch, couple_root, couple_branch, couple_leaf):
    up2 = lift_leaf.transpose(1, 2, 0).reshape(16, 128)
    up1 = lift_branch.reshape(64, 16)
    keep4 = (1.0 - jnp.eye(4, dtype=F32))[:, :, None, None]
    keep8 = (1.0 - jnp.eye(8, dtype=F32))[:, :, None, None]
    root = (couple_root * keep4).transpose(0, 2, 1, 3).reshape(64, 64)
    mid = [lift_branch.transpose(0, 2, 1).reshape(64, 16)]
    for shift in range(1, 4):
        mid.append(jnp.stack([couple_branch[b, (b + shift) % 4] for b in range(4)]).reshape(64, 16))
    mid = jnp.concatenate(mid, axis=1)
    low = (couple_leaf * keep8).transpose(2, 0, 3, 1).reshape(128, 128)
    lift = lift_leaf.transpose(2, 0, 1).reshape(128, 16)
    return up2, up1, root, mid, jnp.concatenate([low, lift], axis=1)


def degree_table():
    table = np.zeros((640, 128), np.float32)
    for group, pair in enumerate(PATTERN):
        for half, degree in enumerate(pair):
            table[group * 128 + half * 64 : group * 128 + (half + 1) * 64, degree::4] = 1.0
    return jnp.asarray(table, BF16)


def swap(x):
    return lax.all_to_all(x, AXES, split_axis=0, concat_axis=0, tiled=True)


def shards(
    features,
    cotangent,
    leaf_device,
    neighbours,
    radial,
    first_zero,
    first_one,
    first_two,
    first_three,
    second_zero,
    second_one,
    second_two,
    second_three,
    lift_leaf,
    lift_branch,
    couple_root,
    couple_branch,
    couple_leaf,
):
    send = pack(leaf_device, features, cotangent)
    got = swap(send.reshape(128, 8, WIDTH))
    nbr = jnp.pad(neighbours.T, ((0, 0), (0, 112)))
    rad = jnp.pad(radial.T, ((0, 0), (0, 64)))
    firsts = (first_zero, first_one, first_two, first_three)
    seconds = (second_zero, second_one, second_two, second_three)
    gu, back, fc, perm, m = leaf_a(
        got.reshape(64, 2, 8, WIDTH),
        nbr,
        rad,
        blocks(firsts, 0.5, False),
        blocks(seconds, 1.0, False),
        blocks(seconds, 1.0, True),
    )
    ret = swap(back.reshape(128, 8, 640))
    grads = leaf_b(gu, fc, perm, m, blocks(firsts, 0.5, True), degree_table())
    mats = tree_mats(lift_leaf, lift_branch, couple_root, couple_branch, couple_leaf)
    updated = finish(ret.reshape(1024, 640), features, leaf_device, mats)
    return updated, grads


def solution(mesh):
    spread = P(AXES, None)
    across = P(None, AXES)
    return jax.shard_map(
        shards,
        mesh=mesh,
        in_specs=(spread, spread, spread, across, across) + (P(),) * 13,
        out_specs=(spread, across),
        check_vma=False,
    )
```

```python
import math

import jax
import jax.numpy as jnp
import numpy as np
from jax import lax
from jax.experimental import pallas as pl
from jax.experimental.pallas import tpu as pltpu
from jax.sharding import PartitionSpec as P

BF16 = jnp.bfloat16
F32 = jnp.float32
AXES = ("gx", "gy", "gz")
EMPTY = 1024.0
ROWS = 256
POOL = 512
WIDTH = 1024
NBR = 16
TILE = 256


def dot(a, b, **kw):
    return jnp.dot(a, b, preferred_element_type=F32, **kw)


def iota(shape, axis):
    return lax.broadcasted_iota(jnp.int32, shape, axis)


def col_of(row):
    n = row.shape[1]
    diag = jnp.where(iota((n, n), 0) == iota((n, n), 1), row.astype(F32), 0.0).astype(BF16)
    return dot(diag, jnp.ones((n, 128), BF16)).astype(jnp.int32)


def split(x):
    high = x.astype(BF16)
    return high, (x - high.astype(F32)).astype(BF16)


def pack_kernel(leaf_ref, feat_ref, grad_ref, send_ref):
    row = leaf_ref[...]
    col = col_of(row)[:, 0:1]
    n = ROWS
    same = (col == row) & (iota((n, n), 0) < iota((n, n), 1))
    rank = jnp.sum(jnp.where(same, 1.0, 0.0), axis=0, keepdims=True).astype(jnp.int32)
    slot = row * 8 + rank
    ones = jnp.ones((n, 128), BF16)
    for part in range(4):
        index = iota((n, n), 0) + part * n
        pick_f = jnp.where(index == slot, 1.0, 0.0).astype(BF16)
        pick_g = jnp.where(index == slot + 4, 1.0, 0.0).astype(BF16)
        there = dot(pick_f, ones)
        gone = (there < 0.5) & ((iota((n, 128), 0) & 7) < 4)
        out = dot(pick_f, feat_ref[...]) + dot(pick_g, grad_ref[...])
        send_ref[part * n : (part + 1) * n, 128:] = out[:, 128:].astype(BF16)
        send_ref[part * n : (part + 1) * n, :128] = jnp.where(gone, EMPTY, out[:, :128]).astype(BF16)


def pack(leaf_row, features, cotangent):
    return pl.pallas_call(
        pack_kernel,
        out_shape=jax.ShapeDtypeStruct((128 * 8, WIDTH), BF16),
        name="pack",
    )(leaf_row, features, cotangent)


def mix(x, w0, w1a, w1b, w2, w3):
    a = dot(x[:, 0:256], w0)
    b = dot(x[:, 256:512], w1a)
    c = dot(x[:, 384:640], w1b)
    d = dot(x[:, 640:896], w2)
    e = dot(x[:, 896:1024], w3)
    return [
        a[:, :128],
        a[:, 128:],
        b[:, :128],
        b[:, 128:] + c[:, :128],
        c[:, 128:],
        d[:, :128],
        d[:, 128:],
        e,
    ]


def gather(index, own_ref, table_ref, out_ref, first, last, tiled):
    for i in range(first, last):
        start = pl.multiple_of(index[i >> 7, i & 127], 8)
        row = own_ref[i * 8 : (i + 1) * 8, :] + table_ref[pl.ds(start, 8), :]
        if tiled:
            out_ref[i >> 3, pl.ds(i & 7, 8, stride=8), :] = row
        else:
            out_ref[i * 8 : (i + 1) * 8, :] = row


def fetch(index_ref, k, index_smem, sem):
    return pltpu.make_async_copy(index_ref.at[jnp.minimum(k, NBR - 1)], index_smem, sem)


def scales(rad_ref, rows, k):
    size = rows.size
    shifted = pltpu.roll(rad_ref[rows, :], (128 - 4 * k) % 128, 1)
    r0, r1, r2, r3 = [jnp.broadcast_to(shifted[:, j : j + 1], (size, 128)) for j in range(4)]
    low = iota((size, 128), 1) < 64
    p01 = jnp.where(low, r0, r1)
    p23 = jnp.where(low, r2, r3)
    p12 = jnp.where(low, r1, r2)
    p31 = jnp.where(low, r3, r1)
    return [p01, p23, p12, p31, p23, p23, p23, r3]


def mix_blocks(piece, w0, w1a, w1b, w2, w3, use):
    out = dot(jnp.concatenate([piece(0), piece(1)], axis=1), w0[...])
    use(0, out[:, :128])
    use(1, out[:, 128:])
    middle = piece(3)
    a = dot(jnp.concatenate([piece(2), middle], axis=1), w1a[...])
    b = dot(jnp.concatenate([middle, piece(4)], axis=1), w1b[...])
    use(2, a[:, :128])
    use(3, a[:, 128:] + b[:, :128])
    use(4, b[:, 128:])
    out = dot(jnp.concatenate([piece(5), piece(6)], axis=1), w2[...])
    use(5, out[:, :128])
    use(6, out[:, 128:])
    use(7, dot(piece(7), w3[...]))


def leaf_a_kernel(
    got_ref,
    nbr_ref,
    rad_ref,
    f0, f1a, f1b, f2, f3,
    s0, s1a, s1b, s2, s3,
    u_ref,
    back_ref,
    own_ref,
    table_ref,
    index_ref,
    occ_ref,
    acc_ref,
    tile_ref,
    buf0_ref,
    buf1_ref,
    rank_ref,
    rank_smem,
    first_smem,
    odd_smem,
    even_smem,
    sem0,
    sem1,
    sem2,
    sem3,
):
    step = pl.program_id(0)

    @pl.when(step == 0)
    def _():
        first = jnp.where(iota((8, 128), 1) == 0, 1.0, 0.0).astype(BF16)
        got0 = got_ref[:, :, :, 0:128].reshape(1024, 128)
        lead = lax.dot_general(first, got0, (((1,), (1,)), ((), ())), preferred_element_type=F32)
        lane = iota((8, 1024), 1)
        occ = jnp.where((lead < 0.5 * EMPTY) & ((lane & 7) < 4), 1.0, 0.0)
        occ8 = jnp.concatenate([occ[0:1, r * 128 : (r + 1) * 128] for r in range(8)], axis=0)
        occ_ref[...] = occ8
        occ8_low = occ8.astype(BF16)
        before = jnp.where(iota((128, 128), 0) < iota((128, 128), 1), 1.0, 0.0).astype(BF16)
        sums = dot(occ8_low, jnp.ones((128, 128), BF16))
        above = jnp.where(iota((8, 8), 1) < iota((8, 8), 0), 1.0, 0.0).astype(BF16)
        rank = dot(occ8_low, before) + dot(above, sums.astype(BF16))
        filled = jnp.sum(sums, axis=0, keepdims=True)
        rank_ref[...] = 8 * jnp.where(occ8 > 0.5, rank, float(POOL)).astype(jnp.int32)
        to_smem = pltpu.make_async_copy(rank_ref, rank_smem, sem0)
        to_smem.start()
        choice = nbr_ref[...].astype(F32)
        filled = jnp.concatenate([filled] * 4, axis=1)
        left = choice - jnp.floor(choice / filled) * filled
        left = jnp.where(left < 0.0, left + filled, left)
        left = 8 * jnp.where(left >= filled, left - filled, left).astype(jnp.int32)
        for r in range(4):
            index_ref[:, r, :] = left[:, r * 128 : (r + 1) * 128]
        fetch(index_ref, 0, first_smem, sem1).start()
        fetch(index_ref, 1, odd_smem, sem2).start()
        fetch(index_ref, 2, even_smem, sem3).start()
        sums = dot(occ.astype(BF16), got_ref[...].reshape(1024, WIDTH))
        tile_ref[...] = sums * (1.0 / math.sqrt(ROWS))
        for pair in range(64):
            for half in range(2):
                block = got_ref[pair, half].astype(F32)
                at = (pair * 2 + half) * 4
                for g in range(8):
                    own_ref[pl.ds(at * 8 + g, 4, stride=8), :] = block[0:4, g * 128 : (g + 1) * 128]
        acc_ref[...] = jnp.zeros_like(acc_ref)
        to_smem.wait()
        for i in range(POOL):
            s = (i >> 2) * 8 + (i & 3)
            to = pl.multiple_of(rank_smem[s >> 7, s & 127], 8)
            table_ref[pl.ds(to, 8), :] = own_ref[i * 8 : (i + 1) * 8, :]
        fetch(index_ref, 0, first_smem, sem1).wait()
        gather(first_smem, own_ref, table_ref, buf0_ref, 0, POOL, False)

    turns = ((buf0_ref, buf1_ref, odd_smem, sem2), (buf1_ref, buf0_ref, even_smem, sem3))
    for half, (buf, other, index_smem, sem) in enumerate(turns):
        k = step * 2 + half
        fetch(index_ref, k + 1, index_smem, sem).wait()
        for part in range(POOL // TILE):
            rows = pl.ds(part * TILE, TILE)
            gather(index_smem, own_ref, table_ref, other, part * TILE, (part + 1) * TILE, False)
            pats = scales(rad_ref, rows, k)

            def piece(g):
                y = buf[pl.ds(part * TILE * 8 + g, TILE, stride=8), :]
                return (y * pats[g]).astype(BF16)

            def use(g, w):
                cols = slice(g * 128, (g + 1) * 128)
                acc_ref[rows, cols] += w + w * jnp.tanh(w)
                u_ref[half, rows, cols] = w

            mix_blocks(piece, f0, f1a, f1b, f2, f3, use)

        @pl.when(step < NBR // 2 - 1)
        def _():
            fetch(index_ref, k + 3, index_smem, sem).start()

    @pl.when(step == NBR // 2 - 1)
    def _():
        total = acc_ref[...]
        high, low = split(total)
        wts = (s0[...], s1a[...], s1b[...], s2[...], s3[...])
        near = [0.25 * (a + b) for a, b in zip(mix(high, *wts), mix(low, *wts))]
        half = iota((64, 8, 512), 1) < 4
        lo = jnp.concatenate(near[:4], axis=1)
        hi = jnp.concatenate(near[4:], axis=1)
        lo_r = pltpu.roll(lo.reshape(64, 8, 512), 4, 1)
        hi_r = pltpu.roll(hi.reshape(64, 8, 512), 4, 1)
        lo = lo.reshape(64, 8, 512)
        hi = hi.reshape(64, 8, 512)
        back_ref[:, 0, :, :512] = jnp.where(half, lo, hi_r).astype(BF16)
        back_ref[:, 1, :, :512] = jnp.where(half, lo_r, hi).astype(BF16)
        tile = tile_ref[...]
        body = jnp.concatenate([tile[0:1, r * 128 : (r + 1) * 128] for r in range(8)], axis=0)
        body = jnp.broadcast_to(body[None, None], (64, 2, 8, 128)).astype(BF16)
        back_ref[:, :, :, 512:] = body


def full(x):
    return pl.BlockSpec(x.shape, lambda k, n=len(x.shape): (0,) * n)


def leaf_a(got, nbr, rad, firsts, seconds):
    args = (got, nbr, rad, *firsts, *seconds)
    out_shape = [
        jax.ShapeDtypeStruct((NBR, POOL, WIDTH), F32),
        jax.ShapeDtypeStruct((64, 2, 8, 640), BF16),
        jax.ShapeDtypeStruct((POOL * 8, 128), F32),
        jax.ShapeDtypeStruct((POOL * 8 + 8, 128), F32),
        jax.ShapeDtypeStruct((NBR, 4, 128), jnp.int32),
        jax.ShapeDtypeStruct((8, 128), F32),
    ]
    return pl.pallas_call(
        leaf_a_kernel,
        grid=(NBR // 2,),
        in_specs=[full(x) for x in args],
        out_specs=[pl.BlockSpec((2, POOL, WIDTH), lambda k: (k, 0, 0))] + [full(x) for x in out_shape[1:]],
        out_shape=out_shape,
        scratch_shapes=[
            pltpu.VMEM((POOL, WIDTH), F32),
            pltpu.VMEM((8, WIDTH), F32),
            pltpu.VMEM((POOL * 8, 128), F32),
            pltpu.VMEM((POOL * 8, 128), F32),
            pltpu.VMEM((8, 128), jnp.int32),
            pltpu.SMEM((8, 128), jnp.int32),
            pltpu.SMEM((4, 128), jnp.int32),
            pltpu.SMEM((4, 128), jnp.int32),
            pltpu.SMEM((4, 128), jnp.int32),
            pltpu.SemaphoreType.DMA,
            pltpu.SemaphoreType.DMA,
            pltpu.SemaphoreType.DMA,
            pltpu.SemaphoreType.DMA,
        ],
        compiler_params=pltpu.CompilerParams(vmem_limit_bytes=56 << 20),
        cost_estimate=pl.CostEstimate(flops=6 << 30, bytes_accessed=24 << 20, transcendentals=8 << 20),
        name="leaf_a",
    )(*args)


def leaf_b_kernel(
    index_ref, u_ref, got_ref, own_ref, table_ref, occ_ref,
    t0, t1a, t1b, t2, t3,
    s0, s1a, s1b, s2, s3,
    sum_ref, out_ref, acc_ref, half_t_ref, buf0_ref, buf1_ref,
    first_smem, odd_smem, even_smem, sem1, sem2, sem3,
):
    step = pl.program_id(0)

    @pl.when(step == 0)
    def _():
        fetch(index_ref, 0, first_smem, sem1).start()
        fetch(index_ref, 1, odd_smem, sem2).start()
        fetch(index_ref, 2, even_smem, sem3).start()
        acc_ref[...] = jnp.zeros_like(acc_ref)
        top = iota((8, WIDTH), 0) < 4
        for part in range(POOL // TILE):
            grad = []
            for pair in range(part * TILE // 8, (part + 1) * TILE // 8):
                a = pltpu.roll(got_ref[pair, 0].astype(F32), 4, 0)
                grad.append(jnp.where(top, a, got_ref[pair, 1].astype(F32)))
            grad = jnp.concatenate(grad, axis=0).astype(BF16)
            rows = slice(part * TILE, (part + 1) * TILE)

            def use(g, value):
                half_t_ref[rows, g * 128 : (g + 1) * 128] = 0.5 * value

            mix_blocks(lambda g: grad[:, g * 128 : (g + 1) * 128], s0, s1a, s1b, s2, s3, use)
        fetch(index_ref, 0, first_smem, sem1).wait()
        gather(first_smem, own_ref, table_ref, buf0_ref, 0, POOL, True)

    turns = ((buf0_ref, buf1_ref, odd_smem, sem2), (buf1_ref, buf0_ref, even_smem, sem3))
    for half, (buf, other, index_smem, sem) in enumerate(turns):
        k = step * 2 + half
        fetch(index_ref, k + 1, index_smem, sem).wait()
        for part in range(POOL // TILE):
            rows = pl.ds(part * TILE, TILE)
            gather(index_smem, own_ref, table_ref, other, part * TILE, (part + 1) * TILE, True)
            prods = {}

            def piece(g):
                cols = slice(g * 128, (g + 1) * 128)
                w = u_ref[half, rows, cols]
                h = jnp.tanh(w)
                up = 1.0 + h
                return ((up + (w * up) * (1.0 - h)) * half_t_ref[rows, cols]).astype(BF16)

            def use(g, s):
                tiles = slice(part * TILE // 8, (part + 1) * TILE // 8)
                prods[g] = s * buf[tiles, g * 8 : (g + 1) * 8, :].reshape(TILE, 128)

            mix_blocks(piece, t0, t1a, t1b, t2, t3, use)
            low = iota((TILE, 128), 1) < 64
            ones = jnp.where(low, prods[2], prods[3])
            ones = ones + pltpu.roll(ones, 64, 1)
            threes = prods[7] + pltpu.roll(prods[7], 64, 1)
            cross = pltpu.roll(jnp.where(low, prods[3], prods[2]), 64, 1)
            x01 = prods[0] + jnp.where(low, 0.0, ones)
            x23 = (prods[1] + prods[4]) + (prods[5] + prods[6]) + cross + jnp.where(low, 0.0, threes)
            sums = dot(jnp.concatenate([x01, x23], axis=1).astype(BF16), sum_ref[...])
            mine = (iota((TILE, 128), 1) >> 2) == k
            acc_ref[rows, :] = jnp.where(mine, sums, acc_ref[rows, :])

        @pl.when(step < NBR // 2 - 1)
        def _():
            fetch(index_ref, k + 3, index_smem, sem).start()

    @pl.when(step == NBR // 2 - 1)
    def _():
        occ = []
        for r in range(8):
            pick = iota((128, 64), 0) == (iota((128, 64), 1) >> 2) * 8 + (iota((128, 64), 1) & 3)
            occ.append(dot(occ_ref[r : r + 1, :].astype(BF16), jnp.where(pick, 1.0, 0.0).astype(BF16)))
        occ = jnp.concatenate(occ, axis=1)
        out_ref[...] = 0.5 * occ * jnp.transpose(acc_ref[...])[0:64, :]


def leaf_b(index, u, got, own, table, occ, trans, seconds_t, sums):
    args = (got, own, table, occ, *trans, *seconds_t, sums)
    return pl.pallas_call(
        leaf_b_kernel,
        grid=(NBR // 2,),
        in_specs=[
            full(index),
            pl.BlockSpec((2, POOL, WIDTH), lambda k: (k, 0, 0)),
        ]
        + [full(x) for x in args],
        out_specs=pl.BlockSpec((64, POOL), lambda k: (0, 0)),
        out_shape=jax.ShapeDtypeStruct((64, POOL), F32),
        scratch_shapes=[
            pltpu.VMEM((POOL, 128), F32),
            pltpu.VMEM((POOL, WIDTH), F32),
            pltpu.VMEM((64, 64, 128), F32),
            pltpu.VMEM((64, 64, 128), F32),
            pltpu.SMEM((4, 128), jnp.int32),
            pltpu.SMEM((4, 128), jnp.int32),
            pltpu.SMEM((4, 128), jnp.int32),
            pltpu.SemaphoreType.DMA,
            pltpu.SemaphoreType.DMA,
            pltpu.SemaphoreType.DMA,
        ],
        compiler_params=pltpu.CompilerParams(vmem_limit_bytes=48 << 20),
        cost_estimate=pl.CostEstimate(flops=6 << 30, bytes_accessed=24 << 20, transcendentals=8 << 20),
        name="leaf_b",
    )(index, u, *args)


def block_swap(tiles):
    low = iota((8, 128), 1) < 64
    out = [[None] * 8 for _ in range(16)]
    for pair in range(8):
        for g in range(8):
            a, b = tiles[2 * pair][g], tiles[2 * pair + 1][g]
            out[2 * g][pair] = jnp.where(low, a, pltpu.roll(b, 64, 1))
            out[2 * g + 1][pair] = jnp.where(low, pltpu.roll(a, 64, 1), b)
    return out


def own_block(x):
    which = (iota((16, 1024), 1) >> 6) & 3
    out = x[0:16]
    for b in range(1, 4):
        out = jnp.where(which == b, x[b * 16 : (b + 1) * 16], out)
    return out


def dot2(a, b):
    high, low = split(a)
    return dot(high, b) + dot(low, b)


def dot3(a, b):
    high, low = split(b)
    return dot2(a, high) + dot(a.astype(BF16), low)


def finish_kernel(ret_ref, feat_ref, leaf_ref, up2_ref, up1_ref, root_ref, mid_ref, low_ref, out_ref, tile_ref):
    tile_ref[...] = ret_ref[:, 512:640].astype(F32)
    tiles = [[tile_ref[pl.ds(ab * 64 + g, 8, stride=8), :] for g in range(8)] for ab in range(16)]
    swapped = block_swap(tiles)
    s2 = jnp.concatenate([jnp.concatenate(row, axis=1) for row in swapped], axis=0)
    s2 = s2.astype(BF16)
    m2 = dot2(up2_ref[...], s2)
    v = own_block(dot3(up1_ref[...], m2))
    parts = []
    for a in range(4):
        s = v[:, a * 256 : a * 256 + 128] + v[:, a * 256 + 128 : a * 256 + 256]
        s = s + pltpu.roll(s, 64, 1)
        parts.append(jnp.concatenate([s, s], axis=1))
    m1 = jnp.concatenate(parts, axis=0)
    l1 = dot3(root_ref[...], m1)
    l1 = jnp.concatenate([l1[a * 16 : (a + 1) * 16] for a in range(4)], axis=1)
    stack = [l1]
    for shift in range(1, 4):
        stack.append(
            jnp.concatenate(
                [pltpu.roll(m2[:, a * 256 : (a + 1) * 256], 256 - 64 * shift, 1) for a in range(4)], axis=1
            )
        )
    l2 = own_block(dot3(mid_ref[...], jnp.concatenate(stack, axis=0)))
    l3 = dot2(low_ref[:, :128], s2) + dot3(low_ref[:, 128:144], l2)
    swapped = block_swap([[l3[q * 8 : (q + 1) * 8, g * 128 : (g + 1) * 128] for g in range(8)] for q in range(16)])
    l3 = jnp.concatenate([jnp.concatenate(row, axis=1) for row in swapped], axis=0)
    l3_high, l3_low = split(l3)

    n = ROWS
    row = leaf_ref[...]
    col = col_of(row)[:, 0:1]
    same = jnp.where((col == row) & (iota((n, n), 1) < iota((n, n), 0)), 1.0, 0.0).astype(BF16)
    rank = dot(same, jnp.ones((n, 128), BF16))[:, 0:1].astype(jnp.int32)
    slot = col * 8 + rank
    lane = iota((n, 1024), 1)
    near_lo = dot(jnp.where(lane == slot, 1.0, 0.0).astype(BF16), ret_ref[:, :512])
    near_hi = dot(jnp.where(lane == slot + 4, 1.0, 0.0).astype(BF16), ret_ref[:, :512])
    mine = jnp.where(iota((n, 128), 1) == col, 1.0, 0.0).astype(BF16)
    local = dot(mine, l3_high) + dot(mine, l3_low)
    feat = feat_ref[...].astype(F32)
    near = jnp.concatenate([near_lo, near_hi], axis=1)
    out_ref[...] = (feat + near + feat * local).astype(BF16)


def finish(ret, features, leaf_row, mats):
    return pl.pallas_call(
        finish_kernel,
        out_shape=jax.ShapeDtypeStruct((ROWS, WIDTH), BF16),
        scratch_shapes=[pltpu.VMEM((1024, 128), F32)],
        name="finish",
    )(ret, features, leaf_row, *mats)


def blocks(mats, scale, flip):
    m0, m1, m2, m3 = [(m.T if flip else m) * jnp.asarray(scale, m.dtype) for m in mats]
    w1a = jnp.pad(m1, ((0, 64), (0, 64)))
    w1b = jnp.pad(m1, ((64, 0), (64, 0)))
    w2 = jnp.pad(m2, ((0, 128), (0, 128))) + jnp.pad(m2, ((128, 0), (128, 0)))
    w3 = jnp.pad(m3, ((0, 64), (0, 64))) + jnp.pad(m3, ((64, 0), (64, 0)))
    return m0, w1a, w1b, w2, w3


def tree_mats(lift_leaf, lift_branch, couple_root, couple_branch, couple_leaf):
    up2 = lift_leaf.transpose(1, 2, 0).reshape(16, 128)
    up1 = lift_branch.reshape(64, 16)
    keep4 = (1.0 - jnp.eye(4, dtype=F32))[:, :, None, None]
    keep8 = (1.0 - jnp.eye(8, dtype=F32))[:, :, None, None]
    root = (couple_root * keep4).transpose(0, 2, 1, 3).reshape(64, 64)
    mid = [lift_branch.transpose(0, 2, 1).reshape(64, 16)]
    for shift in range(1, 4):
        mid.append(jnp.stack([couple_branch[b, (b + shift) % 4] for b in range(4)]).reshape(64, 16))
    mid = jnp.concatenate(mid, axis=1)
    low = (couple_leaf * keep8).transpose(2, 0, 3, 1).reshape(128, 128)
    lift = lift_leaf.transpose(2, 0, 1).reshape(128, 16)
    return up2, up1, root, mid, jnp.concatenate([low, lift], axis=1)


def degree_table():
    table = np.zeros((256, 128), np.float32)
    for degree in range(4):
        table[degree * 64 : (degree + 1) * 64, degree::4] = 1.0
    return jnp.asarray(table, BF16)


def swap(x):
    return lax.all_to_all(x, AXES, split_axis=0, concat_axis=0, tiled=True)


def shards(
    features,
    cotangent,
    leaf_device,
    neighbours,
    radial,
    first_zero,
    first_one,
    first_two,
    first_three,
    second_zero,
    second_one,
    second_two,
    second_three,
    lift_leaf,
    lift_branch,
    couple_root,
    couple_branch,
    couple_leaf,
):
    leaf_row = leaf_device.reshape(1, ROWS)
    send = pack(leaf_row, features, cotangent)
    got = swap(send.reshape(128, 8, WIDTH))
    rad = jnp.pad(radial.T, ((0, 0), (0, 64)))
    firsts = (first_zero, first_one, first_two, first_three)
    seconds = (second_zero, second_one, second_two, second_three)
    got = got.reshape(64, 2, 8, WIDTH)
    u, back, own, table, index, occ = leaf_a(
        got, neighbours, rad, blocks(firsts, 0.5, False), blocks(seconds, 1.0, False)
    )
    ret = swap(back.reshape(128, 8, 640))
    grads = leaf_b(
        index, u, got, own, table, occ, blocks(firsts, 0.5, True), blocks(seconds, 1.0, True), degree_table()
    )
    mats = tree_mats(lift_leaf, lift_branch, couple_root, couple_branch, couple_leaf)
    updated = finish(ret.reshape(1024, 640), features, leaf_row, mats)
    return updated, grads


def solution(mesh):
    spread = P(AXES, None)
    across = P(None, AXES)
    return jax.shard_map(
        shards,
        mesh=mesh,
        in_specs=(spread, spread, spread, across, across) + (P(),) * 13,
        out_specs=(spread, across),
        check_vma=False,
    )
```

```python
import math

import jax
import jax.numpy as jnp
import numpy as np
from jax import lax
from jax.experimental import pallas as pl
from jax.experimental.pallas import tpu as pltpu
from jax.sharding import PartitionSpec as P

BF16 = jnp.bfloat16
F32 = jnp.float32
AXES = ("gx", "gy", "gz")
EMPTY = 1024.0
ROWS = 256
POOL = 512
WIDTH = 1024
NBR = 16
TILE = 128


def dot(a, b, **kw):
    return jnp.dot(a, b, preferred_element_type=F32, **kw)


def iota(shape, axis):
    return lax.broadcasted_iota(jnp.int32, shape, axis)


def col_of(row):
    n = row.shape[1]
    diag = jnp.where(iota((n, n), 0) == iota((n, n), 1), row.astype(F32), 0.0).astype(BF16)
    return dot(diag, jnp.ones((n, 128), BF16)).astype(jnp.int32)


def split(x):
    high = x.astype(BF16)
    return high, (x - high.astype(F32)).astype(BF16)


def pack_kernel(leaf_ref, feat_ref, grad_ref, send_ref):
    row = leaf_ref[...]
    col = col_of(row)[:, 0:1]
    n = ROWS
    same = (col == row) & (iota((n, n), 0) < iota((n, n), 1))
    rank = jnp.sum(jnp.where(same, 1.0, 0.0), axis=0, keepdims=True).astype(jnp.int32)
    slot = row * 8 + rank
    ones = jnp.ones((n, 128), BF16)
    for part in range(4):
        index = iota((n, n), 0) + part * n
        pick_f = jnp.where(index == slot, 1.0, 0.0).astype(BF16)
        pick_g = jnp.where(index == slot + 4, 1.0, 0.0).astype(BF16)
        there = dot(pick_f, ones)
        gone = (there < 0.5) & ((iota((n, 128), 0) & 7) < 4)
        out = dot(pick_f, feat_ref[...]) + dot(pick_g, grad_ref[...])
        send_ref[part * n : (part + 1) * n, 128:] = out[:, 128:].astype(BF16)
        send_ref[part * n : (part + 1) * n, :128] = jnp.where(gone, EMPTY, out[:, :128]).astype(BF16)


def pack(leaf_row, features, cotangent):
    return pl.pallas_call(
        pack_kernel,
        out_shape=jax.ShapeDtypeStruct((128 * 8, WIDTH), BF16),
        name="pack",
    )(leaf_row, features, cotangent)


def mix(x, w0, w1a, w1b, w2, w3):
    a = dot(x[:, 0:256], w0)
    b = dot(x[:, 256:512], w1a)
    c = dot(x[:, 384:640], w1b)
    d = dot(x[:, 640:896], w2)
    e = dot(x[:, 896:1024], w3)
    return [
        a[:, :128],
        a[:, 128:],
        b[:, :128],
        b[:, 128:] + c[:, :128],
        c[:, 128:],
        d[:, :128],
        d[:, 128:],
        e,
    ]


def gather(index_ref, pair, part, own_ref, table_ref, out_ref):
    index = [index_ref.at[2 * pair], index_ref.at[2 * pair + 1]]
    for j in range(TILE):
        i = part * TILE + j
        own = own_ref[i * 8 : (i + 1) * 8, :]
        for which in range(2):
            start = pl.multiple_of(index[which][i >> 7, i & 127], 8)
            row = own + table_ref[pl.ds(start, 8), :]
            out_ref[(which * TILE + j) >> 3, pl.ds(j & 7, 8, stride=8), :] = row


def both(a, b):
    return jnp.concatenate([a, b], axis=0)


def scales(rad_ref, rows, pair):
    shifted = pltpu.roll(rad_ref[rows, :], (128 - 8 * pair) % 128, 1)
    r = [jnp.broadcast_to(shifted[:, j : j + 1], (TILE, 128)) for j in range(8)]
    r0, r1, r2, r3 = [both(r[j], r[j + 4]) for j in range(4)]
    low = iota((2 * TILE, 128), 1) < 64
    p01 = jnp.where(low, r0, r1)
    p23 = jnp.where(low, r2, r3)
    p12 = jnp.where(low, r1, r2)
    p31 = jnp.where(low, r3, r1)
    return [p01, p23, p12, p31, p23, p23, p23, r3]


def mix_blocks(piece, w0, w1a, w1b, w2, w3, use):
    out = dot(jnp.concatenate([piece(0), piece(1)], axis=1), w0[...])
    use(0, out[:, :128])
    use(1, out[:, 128:])
    middle = piece(3)
    a = dot(jnp.concatenate([piece(2), middle], axis=1), w1a[...])
    b = dot(jnp.concatenate([middle, piece(4)], axis=1), w1b[...])
    use(2, a[:, :128])
    use(3, a[:, 128:] + b[:, :128])
    use(4, b[:, 128:])
    out = dot(jnp.concatenate([piece(5), piece(6)], axis=1), w2[...])
    use(5, out[:, :128])
    use(6, out[:, 128:])
    use(7, dot(piece(7), w3[...]))


def leaf_a_kernel(
    got_ref,
    nbr_ref,
    rad_ref,
    f0, f1a, f1b, f2, f3,
    s0, s1a, s1b, s2, s3,
    u_ref,
    back_ref,
    own_ref,
    table_ref,
    index_ref,
    occ_ref,
    acc_ref,
    tile_ref,
    buf0,
    buf1,
    buf2,
    buf3,
    rank_ref,
    rank_smem,
    index_smem,
    sem0,
    sem1,
):
    step = pl.program_id(0)

    @pl.when(step == 0)
    def _():
        first = jnp.where(iota((8, 128), 1) == 0, 1.0, 0.0).astype(BF16)
        got0 = got_ref[:, :, :, 0:128].reshape(1024, 128)
        lead = lax.dot_general(first, got0, (((1,), (1,)), ((), ())), preferred_element_type=F32)
        lane = iota((8, 1024), 1)
        occ = jnp.where((lead < 0.5 * EMPTY) & ((lane & 7) < 4), 1.0, 0.0)
        occ8 = jnp.concatenate([occ[0:1, r * 128 : (r + 1) * 128] for r in range(8)], axis=0)
        occ_ref[...] = occ8
        occ8_low = occ8.astype(BF16)
        before = jnp.where(iota((128, 128), 0) < iota((128, 128), 1), 1.0, 0.0).astype(BF16)
        sums = dot(occ8_low, jnp.ones((128, 128), BF16))
        above = jnp.where(iota((8, 8), 1) < iota((8, 8), 0), 1.0, 0.0).astype(BF16)
        rank = dot(occ8_low, before) + dot(above, sums.astype(BF16))
        filled = jnp.sum(sums, axis=0, keepdims=True)
        rank_ref[...] = 8 * jnp.where(occ8 > 0.5, rank, float(POOL)).astype(jnp.int32)
        to_smem = pltpu.make_async_copy(rank_ref, rank_smem, sem0)
        to_smem.start()
        choice = nbr_ref[...].astype(F32)
        filled = jnp.concatenate([filled] * 4, axis=1)
        left = choice - jnp.floor(choice / filled) * filled
        left = jnp.where(left < 0.0, left + filled, left)
        left = 8 * jnp.where(left >= filled, left - filled, left).astype(jnp.int32)
        for r in range(4):
            index_ref[:, r, :] = left[:, r * 128 : (r + 1) * 128]
        index_to_smem = pltpu.make_async_copy(index_ref, index_smem, sem1)
        index_to_smem.start()
        sums = dot(occ.astype(BF16), got_ref[...].reshape(1024, WIDTH))
        tile_ref[...] = sums * (1.0 / math.sqrt(ROWS))
        for pair in range(64):
            for half in range(2):
                block = got_ref[pair, half].astype(F32)
                at = (pair * 2 + half) * 4
                for g in range(8):
                    own_ref[pl.ds(at * 8 + g, 4, stride=8), :] = block[0:4, g * 128 : (g + 1) * 128]
        acc_ref[...] = jnp.zeros_like(acc_ref)
        to_smem.wait()
        for i in range(POOL):
            s = (i >> 2) * 8 + (i & 3)
            to = pl.multiple_of(rank_smem[s >> 7, s & 127], 8)
            table_ref[pl.ds(to, 8), :] = own_ref[i * 8 : (i + 1) * 8, :]
        index_to_smem.wait()
        gather(index_smem, 0, 0, own_ref, table_ref, buf0)

    bufs = (buf0, buf1, buf2, buf3)
    for turn in range(4):
        after = jnp.minimum(step + (turn + 1) // 4, NBR // 2 - 1)
        gather(index_smem, after, (turn + 1) % 4, own_ref, table_ref, bufs[(turn + 1) % 4])
        rows = pl.ds(turn * TILE, TILE)
        pats = scales(rad_ref, rows, step)

        def piece(g):
            y = bufs[turn][:, g * 8 : (g + 1) * 8, :].reshape(2 * TILE, 128)
            return (y * pats[g]).astype(BF16)

        def use(g, w):
            cols = slice(g * 128, (g + 1) * 128)
            v = w + w * jnp.tanh(w)
            acc_ref[rows, cols] += v[:TILE] + v[TILE:]
            u_ref[0, rows, cols] = w[:TILE]
            u_ref[1, rows, cols] = w[TILE:]

        mix_blocks(piece, f0, f1a, f1b, f2, f3, use)

    @pl.when(step == NBR // 2 - 1)
    def _():
        total = acc_ref[...]
        high, low = split(total)
        wts = (s0[...], s1a[...], s1b[...], s2[...], s3[...])
        near = [0.25 * (a + b) for a, b in zip(mix(high, *wts), mix(low, *wts))]
        half = iota((64, 8, 512), 1) < 4
        lo = jnp.concatenate(near[:4], axis=1)
        hi = jnp.concatenate(near[4:], axis=1)
        lo_r = pltpu.roll(lo.reshape(64, 8, 512), 4, 1)
        hi_r = pltpu.roll(hi.reshape(64, 8, 512), 4, 1)
        lo = lo.reshape(64, 8, 512)
        hi = hi.reshape(64, 8, 512)
        back_ref[:, 0, :, :512] = jnp.where(half, lo, hi_r).astype(BF16)
        back_ref[:, 1, :, :512] = jnp.where(half, lo_r, hi).astype(BF16)
        tile = tile_ref[...]
        body = jnp.concatenate([tile[0:1, r * 128 : (r + 1) * 128] for r in range(8)], axis=0)
        body = jnp.broadcast_to(body[None, None], (64, 2, 8, 128)).astype(BF16)
        back_ref[:, :, :, 512:] = body


WHOLE = pl.BlockSpec(memory_space=pltpu.VMEM)


def leaf_a(got, nbr, rad, firsts, seconds):
    args = (got, nbr, rad, *firsts, *seconds)
    out_shape = [
        jax.ShapeDtypeStruct((NBR, POOL, WIDTH), F32),
        jax.ShapeDtypeStruct((64, 2, 8, 640), BF16),
        jax.ShapeDtypeStruct((POOL * 8, 128), F32),
        jax.ShapeDtypeStruct((POOL * 8 + 8, 128), F32),
        jax.ShapeDtypeStruct((NBR, 4, 128), jnp.int32),
        jax.ShapeDtypeStruct((8, 128), F32),
    ]
    return pl.pallas_call(
        leaf_a_kernel,
        grid=(NBR // 2,),
        in_specs=[WHOLE] * len(args),
        out_specs=[pl.BlockSpec((2, POOL, WIDTH), lambda k: (k, 0, 0))] + [WHOLE] * (len(out_shape) - 1),
        out_shape=out_shape,
        scratch_shapes=[
            pltpu.VMEM((POOL, WIDTH), F32),
            pltpu.VMEM((8, WIDTH), F32),
        ]
        + [pltpu.VMEM((TILE // 4, 64, 128), F32)] * 4
        + [
            pltpu.VMEM((8, 128), jnp.int32),
            pltpu.SMEM((8, 128), jnp.int32),
            pltpu.SMEM((NBR, 4, 128), jnp.int32),
            pltpu.SemaphoreType.DMA,
            pltpu.SemaphoreType.DMA,
        ],
        compiler_params=pltpu.CompilerParams(vmem_limit_bytes=40 << 20),
        cost_estimate=pl.CostEstimate(flops=6 << 30, bytes_accessed=24 << 20, transcendentals=8 << 20),
        name="leaf_a",
    )(*args)


def leaf_b_kernel(
    index_ref, u_ref, got_ref, own_ref, table_ref, occ_ref,
    t0, t1a, t1b, t2, t3,
    s0, s1a, s1b, s2, s3,
    sum_ref, out_ref, acc_ref, half_t_ref, buf0, buf1, buf2, buf3,
):
    step = pl.program_id(0)

    @pl.when(step == 0)
    def _():
        acc_ref[...] = jnp.zeros_like(acc_ref)
        top = iota((8, WIDTH), 0) < 4
        for part in range(POOL // TILE):
            grad = []
            for pair in range(part * TILE // 8, (part + 1) * TILE // 8):
                a = pltpu.roll(got_ref[pair, 0].astype(F32), 4, 0)
                grad.append(jnp.where(top, a, got_ref[pair, 1].astype(F32)))
            grad = jnp.concatenate(grad, axis=0).astype(BF16)
            rows = slice(part * TILE, (part + 1) * TILE)

            def use(g, value):
                half_t_ref[rows, g * 128 : (g + 1) * 128] = 0.5 * value

            mix_blocks(lambda g: grad[:, g * 128 : (g + 1) * 128], s0, s1a, s1b, s2, s3, use)
        gather(index_ref, 0, 0, own_ref, table_ref, buf0)

    bufs = (buf0, buf1, buf2, buf3)
    for turn in range(4):
        after = jnp.minimum(step + (turn + 1) // 4, NBR // 2 - 1)
        gather(index_ref, after, (turn + 1) % 4, own_ref, table_ref, bufs[(turn + 1) % 4])
        rows = pl.ds(turn * TILE, TILE)
        prods = {}

        def piece(g):
            cols = slice(g * 128, (g + 1) * 128)
            half_t = half_t_ref[rows, cols]
            out = []
            for which in range(2):
                w = u_ref[which, rows, cols]
                h = jnp.tanh(w)
                up = 1.0 + h
                out.append(((up + (w * up) * (1.0 - h)) * half_t).astype(BF16))
            return both(*out)

        def use(g, s):
            prods[g] = s * bufs[turn][:, g * 8 : (g + 1) * 8, :].reshape(2 * TILE, 128)

        mix_blocks(piece, t0, t1a, t1b, t2, t3, use)
        low = iota((2 * TILE, 128), 1) < 64
        ones = jnp.where(low, prods[2], prods[3])
        ones = ones + pltpu.roll(ones, 64, 1)
        threes = prods[7] + pltpu.roll(prods[7], 64, 1)
        cross = pltpu.roll(jnp.where(low, prods[3], prods[2]), 64, 1)
        x01 = prods[0] + jnp.where(low, 0.0, ones)
        x23 = (prods[1] + prods[4]) + (prods[5] + prods[6]) + cross + jnp.where(low, 0.0, threes)
        sums = dot(jnp.concatenate([x01, x23], axis=1).astype(BF16), sum_ref[...])
        owner = iota((TILE, 128), 1) >> 2
        kept = jnp.where(owner == 2 * step, sums[:TILE], acc_ref[rows, :])
        acc_ref[rows, :] = jnp.where(owner == 2 * step + 1, sums[TILE:], kept)

    @pl.when(step == NBR // 2 - 1)
    def _():
        occ = []
        for r in range(8):
            pick = iota((128, 64), 0) == (iota((128, 64), 1) >> 2) * 8 + (iota((128, 64), 1) & 3)
            occ.append(dot(occ_ref[r : r + 1, :].astype(BF16), jnp.where(pick, 1.0, 0.0).astype(BF16)))
        occ = jnp.concatenate(occ, axis=1)
        out_ref[...] = 0.5 * occ * jnp.transpose(acc_ref[...])[0:64, :]


def leaf_b(index, u, got, own, table, occ, trans, seconds_t, sums):
    args = (got, own, table, occ, *trans, *seconds_t, sums)
    return pl.pallas_call(
        leaf_b_kernel,
        grid=(NBR // 2,),
        in_specs=[
            pl.BlockSpec(memory_space=pltpu.SMEM),
            pl.BlockSpec((2, POOL, WIDTH), lambda k: (k, 0, 0)),
        ]
        + [WHOLE] * len(args),
        out_specs=pl.BlockSpec((64, POOL), lambda k: (0, 0)),
        out_shape=jax.ShapeDtypeStruct((64, POOL), F32),
        scratch_shapes=[
            pltpu.VMEM((POOL, 128), F32),
            pltpu.VMEM((POOL, WIDTH), F32),
        ]
        + [pltpu.VMEM((TILE // 4, 64, 128), F32)] * 4,
        compiler_params=pltpu.CompilerParams(vmem_limit_bytes=32 << 20),
        cost_estimate=pl.CostEstimate(flops=6 << 30, bytes_accessed=24 << 20, transcendentals=8 << 20),
        name="leaf_b",
    )(index, u, *args)


def block_swap(tiles):
    low = iota((8, 128), 1) < 64
    out = [[None] * 8 for _ in range(16)]
    for pair in range(8):
        for g in range(8):
            a, b = tiles[2 * pair][g], tiles[2 * pair + 1][g]
            out[2 * g][pair] = jnp.where(low, a, pltpu.roll(b, 64, 1))
            out[2 * g + 1][pair] = jnp.where(low, pltpu.roll(a, 64, 1), b)
    return out


def own_block(x):
    which = (iota((16, 1024), 1) >> 6) & 3
    out = x[0:16]
    for b in range(1, 4):
        out = jnp.where(which == b, x[b * 16 : (b + 1) * 16], out)
    return out


def dot2(a, b):
    high, low = split(a)
    return dot(high, b) + dot(low, b)


def dot3(a, b):
    high, low = split(b)
    return dot2(a, high) + dot(a.astype(BF16), low)


def finish_kernel(ret_ref, feat_ref, leaf_ref, up2_ref, up1_ref, root_ref, mid_ref, low_ref, out_ref, tile_ref):
    tile_ref[...] = ret_ref[:, 512:640].astype(F32)
    tiles = [[tile_ref[pl.ds(ab * 64 + g, 8, stride=8), :] for g in range(8)] for ab in range(16)]
    swapped = block_swap(tiles)
    s2 = jnp.concatenate([jnp.concatenate(row, axis=1) for row in swapped], axis=0)
    s2 = s2.astype(BF16)
    m2 = dot2(up2_ref[...], s2)
    v = own_block(dot3(up1_ref[...], m2))
    parts = []
    for a in range(4):
        s = v[:, a * 256 : a * 256 + 128] + v[:, a * 256 + 128 : a * 256 + 256]
        s = s + pltpu.roll(s, 64, 1)
        parts.append(jnp.concatenate([s, s], axis=1))
    m1 = jnp.concatenate(parts, axis=0)
    l1 = dot3(root_ref[...], m1)
    l1 = jnp.concatenate([l1[a * 16 : (a + 1) * 16] for a in range(4)], axis=1)
    stack = [l1]
    for shift in range(1, 4):
        stack.append(
            jnp.concatenate(
                [pltpu.roll(m2[:, a * 256 : (a + 1) * 256], 256 - 64 * shift, 1) for a in range(4)], axis=1
            )
        )
    l2 = own_block(dot3(mid_ref[...], jnp.concatenate(stack, axis=0)))
    l3 = dot2(low_ref[:, :128], s2) + dot3(low_ref[:, 128:144], l2)
    swapped = block_swap([[l3[q * 8 : (q + 1) * 8, g * 128 : (g + 1) * 128] for g in range(8)] for q in range(16)])
    l3 = jnp.concatenate([jnp.concatenate(row, axis=1) for row in swapped], axis=0)
    l3_high, l3_low = split(l3)

    n = ROWS
    row = leaf_ref[...]
    col = col_of(row)[:, 0:1]
    same = jnp.where((col == row) & (iota((n, n), 1) < iota((n, n), 0)), 1.0, 0.0).astype(BF16)
    rank = dot(same, jnp.ones((n, 128), BF16))[:, 0:1].astype(jnp.int32)
    slot = col * 8 + rank
    lane = iota((n, 1024), 1)
    near_lo = dot(jnp.where(lane == slot, 1.0, 0.0).astype(BF16), ret_ref[:, :512])
    near_hi = dot(jnp.where(lane == slot + 4, 1.0, 0.0).astype(BF16), ret_ref[:, :512])
    mine = jnp.where(iota((n, 128), 1) == col, 1.0, 0.0).astype(BF16)
    local = dot(mine, l3_high) + dot(mine, l3_low)
    feat = feat_ref[...].astype(F32)
    near = jnp.concatenate([near_lo, near_hi], axis=1)
    out_ref[...] = (feat + near + feat * local).astype(BF16)


def finish(ret, features, leaf_row, mats):
    return pl.pallas_call(
        finish_kernel,
        out_shape=jax.ShapeDtypeStruct((ROWS, WIDTH), BF16),
        scratch_shapes=[pltpu.VMEM((1024, 128), F32)],
        name="finish",
    )(ret, features, leaf_row, *mats)


def blocks(mats, scale, flip):
    m0, m1, m2, m3 = [(m.T if flip else m) * jnp.asarray(scale, m.dtype) for m in mats]
    w1a = jnp.pad(m1, ((0, 64), (0, 64)))
    w1b = jnp.pad(m1, ((64, 0), (64, 0)))
    w2 = jnp.pad(m2, ((0, 128), (0, 128))) + jnp.pad(m2, ((128, 0), (128, 0)))
    w3 = jnp.pad(m3, ((0, 64), (0, 64))) + jnp.pad(m3, ((64, 0), (64, 0)))
    return m0, w1a, w1b, w2, w3


def tree_mats(lift_leaf, lift_branch, couple_root, couple_branch, couple_leaf):
    up2 = lift_leaf.transpose(1, 2, 0).reshape(16, 128)
    up1 = lift_branch.reshape(64, 16)
    keep4 = (1.0 - jnp.eye(4, dtype=F32))[:, :, None, None]
    keep8 = (1.0 - jnp.eye(8, dtype=F32))[:, :, None, None]
    root = (couple_root * keep4).transpose(0, 2, 1, 3).reshape(64, 64)
    mid = [lift_branch.transpose(0, 2, 1).reshape(64, 16)]
    for shift in range(1, 4):
        mid.append(jnp.stack([couple_branch[b, (b + shift) % 4] for b in range(4)]).reshape(64, 16))
    mid = jnp.concatenate(mid, axis=1)
    low = (couple_leaf * keep8).transpose(2, 0, 3, 1).reshape(128, 128)
    lift = lift_leaf.transpose(2, 0, 1).reshape(128, 16)
    return up2, up1, root, mid, jnp.concatenate([low, lift], axis=1)


def degree_table():
    table = np.zeros((256, 128), np.float32)
    for degree in range(4):
        table[degree * 64 : (degree + 1) * 64, degree::4] = 1.0
    return jnp.asarray(table, BF16)


def swap(x):
    return lax.all_to_all(x, AXES, split_axis=0, concat_axis=0, tiled=True)


def shards(
    features,
    cotangent,
    leaf_device,
    neighbours,
    radial,
    first_zero,
    first_one,
    first_two,
    first_three,
    second_zero,
    second_one,
    second_two,
    second_three,
    lift_leaf,
    lift_branch,
    couple_root,
    couple_branch,
    couple_leaf,
):
    leaf_row = leaf_device.reshape(1, ROWS)
    send = pack(leaf_row, features, cotangent)
    got = swap(send.reshape(128, 8, WIDTH))
    rad = jnp.pad(radial.T, ((0, 0), (0, 64)))
    firsts = (first_zero, first_one, first_two, first_three)
    seconds = (second_zero, second_one, second_two, second_three)
    got = got.reshape(64, 2, 8, WIDTH)
    u, back, own, table, index, occ = leaf_a(
        got, neighbours, rad, blocks(firsts, 0.5, False), blocks(seconds, 1.0, False)
    )
    ret = swap(back.reshape(128, 8, 640))
    grads = leaf_b(
        index, u, got, own, table, occ, blocks(firsts, 0.5, True), blocks(seconds, 1.0, True), degree_table()
    )
    mats = tree_mats(lift_leaf, lift_branch, couple_root, couple_branch, couple_leaf)
    updated = finish(ret.reshape(1024, 640), features, leaf_row, mats)
    return updated, grads


def solution(mesh):
    spread = P(AXES, None)
    across = P(None, AXES)
    return jax.shard_map(
        shards,
        mesh=mesh,
        in_specs=(spread, spread, spread, across, across) + (P(),) * 13,
        out_specs=(spread, across),
        check_vma=False,
    )
```

```python
import math

import jax
import jax.numpy as jnp
import numpy as np
from jax import lax
from jax.experimental import pallas as pl
from jax.experimental.pallas import tpu as pltpu
from jax.sharding import PartitionSpec as P

BF16 = jnp.bfloat16
F32 = jnp.float32
AXES = ("gx", "gy", "gz")
EMPTY = 1024.0
ROWS = 256
POOL = 512
WIDTH = 1024
NBR = 16
TILE = 128


def dot(a, b, **kw):
    return jnp.dot(a, b, preferred_element_type=F32, **kw)


def iota(shape, axis):
    return lax.broadcasted_iota(jnp.int32, shape, axis)


def col_of(row):
    n = row.shape[1]
    diag = jnp.where(iota((n, n), 0) == iota((n, n), 1), row.astype(F32), 0.0).astype(BF16)
    return dot(diag, jnp.ones((n, 128), BF16)).astype(jnp.int32)


def split(x):
    high = x.astype(BF16)
    return high, (x - high.astype(F32)).astype(BF16)


def pack_kernel(leaf_ref, feat_ref, grad_ref, send_ref):
    row = leaf_ref[...]
    col = col_of(row)[:, 0:1]
    n = ROWS
    same = (col == row) & (iota((n, n), 0) < iota((n, n), 1))
    rank = jnp.sum(jnp.where(same, 1.0, 0.0), axis=0, keepdims=True).astype(jnp.int32)
    slot = row * 8 + rank
    ones = jnp.ones((n, 128), BF16)
    for part in range(4):
        index = iota((n, n), 0) + part * n
        pick_f = jnp.where(index == slot, 1.0, 0.0).astype(BF16)
        pick_g = jnp.where(index == slot + 4, 1.0, 0.0).astype(BF16)
        there = dot(pick_f, ones)
        gone = (there < 0.5) & ((iota((n, 128), 0) & 7) < 4)
        out = dot(pick_f, feat_ref[...]) + dot(pick_g, grad_ref[...])
        send_ref[part * n : (part + 1) * n, 128:] = out[:, 128:].astype(BF16)
        send_ref[part * n : (part + 1) * n, :128] = jnp.where(gone, EMPTY, out[:, :128]).astype(BF16)


def pack(leaf_row, features, cotangent):
    return pl.pallas_call(
        pack_kernel,
        out_shape=jax.ShapeDtypeStruct((128 * 8, WIDTH), BF16),
        name="pack",
    )(leaf_row, features, cotangent)


def mix(x, w0, w1a, w1b, w2, w3):
    a = dot(x[:, 0:256], w0)
    b = dot(x[:, 256:512], w1a)
    c = dot(x[:, 384:640], w1b)
    d = dot(x[:, 640:896], w2)
    e = dot(x[:, 896:1024], w3)
    return [
        a[:, :128],
        a[:, 128:],
        b[:, :128],
        b[:, 128:] + c[:, :128],
        c[:, 128:],
        d[:, :128],
        d[:, 128:],
        e,
    ]


def gather(index_ref, pair, part, own_ref, table_ref, out_ref):
    index = [index_ref.at[2 * pair], index_ref.at[2 * pair + 1]]
    for j in range(TILE):
        i = part * TILE + j
        own = own_ref[i * 8 : (i + 1) * 8, :]
        for which in range(2):
            start = pl.multiple_of(index[which][i >> 7, i & 127], 8)
            row = own + table_ref[pl.ds(start, 8), :]
            out_ref[0, part, (which * TILE + j) >> 3, pl.ds(j & 7, 8, stride=8), :] = row


def both(a, b):
    return jnp.concatenate([a, b], axis=0)


def scales(rad_ref, rows, pair):
    shifted = pltpu.roll(rad_ref[rows, :], (128 - 8 * pair) % 128, 1)
    r = [jnp.broadcast_to(shifted[:, j : j + 1], (TILE, 128)) for j in range(8)]
    r0, r1, r2, r3 = [both(r[j], r[j + 4]) for j in range(4)]
    low = iota((2 * TILE, 128), 1) < 64
    p01 = jnp.where(low, r0, r1)
    p23 = jnp.where(low, r2, r3)
    p12 = jnp.where(low, r1, r2)
    p31 = jnp.where(low, r3, r1)
    return [p01, p23, p12, p31, p23, p23, p23, r3]


def mix_blocks(piece, w0, w1a, w1b, w2, w3, use):
    out = dot(jnp.concatenate([piece(0), piece(1)], axis=1), w0[...])
    use(0, out[:, :128])
    use(1, out[:, 128:])
    middle = piece(3)
    a = dot(jnp.concatenate([piece(2), middle], axis=1), w1a[...])
    b = dot(jnp.concatenate([middle, piece(4)], axis=1), w1b[...])
    use(2, a[:, :128])
    use(3, a[:, 128:] + b[:, :128])
    use(4, b[:, 128:])
    out = dot(jnp.concatenate([piece(5), piece(6)], axis=1), w2[...])
    use(5, out[:, :128])
    use(6, out[:, 128:])
    use(7, dot(piece(7), w3[...]))


def leaf_a_kernel(
    got_hbm,
    nbr_ref,
    rad_ref,
    f0, f1a, f1b, f2, f3,
    s0, s1a, s1b, s2, s3,
    u_ref,
    y_ref,
    back_ref,
    occ_ref,
    got_ref,
    own_ref,
    table_ref,
    index_ref,
    acc_ref,
    tile_ref,
    rank_ref,
    rank_smem,
    index_smem,
    sem0,
    sem1,
):
    step = pl.program_id(0)

    @pl.when(step == 0)
    def _():
        pltpu.sync_copy(got_hbm, got_ref)
        first = jnp.where(iota((8, 128), 1) == 0, 1.0, 0.0).astype(BF16)
        got0 = got_ref[:, :, :, 0:128].reshape(1024, 128)
        lead = lax.dot_general(first, got0, (((1,), (1,)), ((), ())), preferred_element_type=F32)
        lane = iota((8, 1024), 1)
        occ = jnp.where((lead < 0.5 * EMPTY) & ((lane & 7) < 4), 1.0, 0.0)
        occ8 = jnp.concatenate([occ[0:1, r * 128 : (r + 1) * 128] for r in range(8)], axis=0)
        occ_ref[...] = occ8
        occ8_low = occ8.astype(BF16)
        before = jnp.where(iota((128, 128), 0) < iota((128, 128), 1), 1.0, 0.0).astype(BF16)
        sums = dot(occ8_low, jnp.ones((128, 128), BF16))
        above = jnp.where(iota((8, 8), 1) < iota((8, 8), 0), 1.0, 0.0).astype(BF16)
        rank = dot(occ8_low, before) + dot(above, sums.astype(BF16))
        filled = jnp.sum(sums, axis=0, keepdims=True)
        rank_ref[...] = 8 * jnp.where(occ8 > 0.5, rank, float(POOL)).astype(jnp.int32)
        to_smem = pltpu.make_async_copy(rank_ref, rank_smem, sem0)
        to_smem.start()
        choice = nbr_ref[...].astype(F32)
        filled = jnp.concatenate([filled] * 4, axis=1)
        left = choice - jnp.floor(choice / filled) * filled
        left = jnp.where(left < 0.0, left + filled, left)
        left = 8 * jnp.where(left >= filled, left - filled, left).astype(jnp.int32)
        for r in range(4):
            index_ref[:, r, :] = left[:, r * 128 : (r + 1) * 128]
        index_to_smem = pltpu.make_async_copy(index_ref, index_smem, sem1)
        index_to_smem.start()
        sums = dot(occ.astype(BF16), got_ref[...].reshape(1024, WIDTH))
        tile_ref[...] = sums * (1.0 / math.sqrt(ROWS))
        for pair in range(64):
            for half in range(2):
                block = got_ref[pair, half].astype(F32)
                at = (pair * 2 + half) * 4
                for g in range(8):
                    own_ref[pl.ds(at * 8 + g, 4, stride=8), :] = block[0:4, g * 128 : (g + 1) * 128]
        acc_ref[...] = jnp.zeros_like(acc_ref)
        to_smem.wait()
        for i in range(POOL):
            s = (i >> 2) * 8 + (i & 3)
            to = pl.multiple_of(rank_smem[s >> 7, s & 127], 8)
            table_ref[pl.ds(to, 8), :] = own_ref[i * 8 : (i + 1) * 8, :]
        index_to_smem.wait()

    gather(index_smem, step, 0, own_ref, table_ref, y_ref)
    for turn in range(4):
        if turn < 3:
            gather(index_smem, step, turn + 1, own_ref, table_ref, y_ref)
        rows = pl.ds(turn * TILE, TILE)
        pats = scales(rad_ref, rows, step)

        def piece(g):
            y = y_ref[0, turn, :, g * 8 : (g + 1) * 8, :].reshape(2 * TILE, 128)
            return (y * pats[g]).astype(BF16)

        def use(g, w):
            cols = slice(g * 128, (g + 1) * 128)
            v = w + w * jnp.tanh(w)
            acc_ref[rows, cols] += v[:TILE] + v[TILE:]
            u_ref[0, rows, cols] = w[:TILE].astype(BF16)
            u_ref[1, rows, cols] = w[TILE:].astype(BF16)

        mix_blocks(piece, f0, f1a, f1b, f2, f3, use)

    @pl.when(step == NBR // 2 - 1)
    def _():
        total = acc_ref[...]
        high, low = split(total)
        wts = (s0[...], s1a[...], s1b[...], s2[...], s3[...])
        near = [0.25 * (a + b) for a, b in zip(mix(high, *wts), mix(low, *wts))]
        half = iota((64, 8, 512), 1) < 4
        lo = jnp.concatenate(near[:4], axis=1)
        hi = jnp.concatenate(near[4:], axis=1)
        lo_r = pltpu.roll(lo.reshape(64, 8, 512), 4, 1)
        hi_r = pltpu.roll(hi.reshape(64, 8, 512), 4, 1)
        lo = lo.reshape(64, 8, 512)
        hi = hi.reshape(64, 8, 512)
        back_ref[:, 0, :, :512] = jnp.where(half, lo, hi_r).astype(BF16)
        back_ref[:, 1, :, :512] = jnp.where(half, lo_r, hi).astype(BF16)
        tile = tile_ref[...]
        body = jnp.concatenate([tile[0:1, r * 128 : (r + 1) * 128] for r in range(8)], axis=0)
        body = jnp.broadcast_to(body[None, None], (64, 2, 8, 128)).astype(BF16)
        back_ref[:, :, :, 512:] = body


def full(x):
    return pl.BlockSpec(x.shape, lambda k, n=len(x.shape): (0,) * n)


HBM = pl.BlockSpec(memory_space=pltpu.HBM)
Y_BLOCK = (1, 4, TILE // 4, 64, 128)


def leaf_a(got, nbr, rad, firsts, seconds):
    args = (nbr, rad, *firsts, *seconds)
    out_shape = [
        jax.ShapeDtypeStruct((NBR, POOL, WIDTH), BF16),
        jax.ShapeDtypeStruct((NBR // 2,) + Y_BLOCK[1:], F32),
        jax.ShapeDtypeStruct((64, 2, 8, 640), BF16),
        jax.ShapeDtypeStruct((8, 128), F32),
    ]
    return pl.pallas_call(
        leaf_a_kernel,
        grid=(NBR // 2,),
        in_specs=[HBM] + [full(x) for x in args],
        out_specs=[
            pl.BlockSpec((2, POOL, WIDTH), lambda k: (k, 0, 0)),
            pl.BlockSpec(Y_BLOCK, lambda k: (k, 0, 0, 0, 0)),
            full(out_shape[2]),
            full(out_shape[3]),
        ],
        out_shape=out_shape,
        scratch_shapes=[
            pltpu.VMEM((64, 2, 8, WIDTH), BF16),
            pltpu.VMEM((POOL * 8, 128), F32),
            pltpu.VMEM((POOL * 8 + 8, 128), F32),
            pltpu.VMEM((NBR, 4, 128), jnp.int32),
            pltpu.VMEM((POOL, WIDTH), F32),
            pltpu.VMEM((8, WIDTH), F32),
            pltpu.VMEM((8, 128), jnp.int32),
            pltpu.SMEM((8, 128), jnp.int32),
            pltpu.SMEM((NBR, 4, 128), jnp.int32),
            pltpu.SemaphoreType.DMA,
            pltpu.SemaphoreType.DMA,
        ],
        compiler_params=pltpu.CompilerParams(vmem_limit_bytes=56 << 20),
        cost_estimate=pl.CostEstimate(flops=6 << 30, bytes_accessed=50 << 20, transcendentals=8 << 20),
        name="leaf_a",
    )(got, *args)


def leaf_b_kernel(
    u_ref, y_ref, got_hbm, occ_ref,
    t0, t1a, t1b, t2, t3,
    s0, s1a, s1b, s2, s3,
    sum_ref, out_ref, acc_ref, half_t_ref, got_ref,
):
    step = pl.program_id(0)

    @pl.when(step == 0)
    def _():
        pltpu.sync_copy(got_hbm, got_ref)
        acc_ref[...] = jnp.zeros_like(acc_ref)
        top = iota((8, WIDTH), 0) < 4
        for part in range(POOL // TILE):
            grad = []
            for pair in range(part * TILE // 8, (part + 1) * TILE // 8):
                a = pltpu.roll(got_ref[pair, 0].astype(F32), 4, 0)
                grad.append(jnp.where(top, a, got_ref[pair, 1].astype(F32)))
            grad = jnp.concatenate(grad, axis=0).astype(BF16)
            rows = slice(part * TILE, (part + 1) * TILE)

            def use(g, value):
                half_t_ref[rows, g * 128 : (g + 1) * 128] = 0.5 * value

            mix_blocks(lambda g: grad[:, g * 128 : (g + 1) * 128], s0, s1a, s1b, s2, s3, use)

    for turn in range(4):
        rows = pl.ds(turn * TILE, TILE)
        prods = {}

        def piece(g):
            cols = slice(g * 128, (g + 1) * 128)
            half_t = half_t_ref[rows, cols]
            out = []
            for which in range(2):
                w = u_ref[which, rows, cols].astype(F32)
                h = jnp.tanh(w)
                up = 1.0 + h
                out.append(((up + (w * up) * (1.0 - h)) * half_t).astype(BF16))
            return both(*out)

        def use(g, s):
            prods[g] = s * y_ref[0, turn, :, g * 8 : (g + 1) * 8, :].reshape(2 * TILE, 128)

        mix_blocks(piece, t0, t1a, t1b, t2, t3, use)
        low = iota((2 * TILE, 128), 1) < 64
        ones = jnp.where(low, prods[2], prods[3])
        ones = ones + pltpu.roll(ones, 64, 1)
        threes = prods[7] + pltpu.roll(prods[7], 64, 1)
        cross = pltpu.roll(jnp.where(low, prods[3], prods[2]), 64, 1)
        x01 = prods[0] + jnp.where(low, 0.0, ones)
        x23 = (prods[1] + prods[4]) + (prods[5] + prods[6]) + cross + jnp.where(low, 0.0, threes)
        sums = dot(jnp.concatenate([x01, x23], axis=1).astype(BF16), sum_ref[...])
        owner = iota((TILE, 128), 1) >> 2
        kept = jnp.where(owner == 2 * step, sums[:TILE], acc_ref[rows, :])
        acc_ref[rows, :] = jnp.where(owner == 2 * step + 1, sums[TILE:], kept)

    @pl.when(step == NBR // 2 - 1)
    def _():
        occ = []
        for r in range(8):
            pick = iota((128, 64), 0) == (iota((128, 64), 1) >> 2) * 8 + (iota((128, 64), 1) & 3)
            occ.append(dot(occ_ref[r : r + 1, :].astype(BF16), jnp.where(pick, 1.0, 0.0).astype(BF16)))
        occ = jnp.concatenate(occ, axis=1)
        out_ref[...] = 0.5 * occ * jnp.transpose(acc_ref[...])[0:64, :]


def leaf_b(u, y, got, occ, firsts_t, seconds_t, sums):
    args = (occ, *firsts_t, *seconds_t, sums)
    return pl.pallas_call(
        leaf_b_kernel,
        grid=(NBR // 2,),
        in_specs=[
            pl.BlockSpec((2, POOL, WIDTH), lambda k: (k, 0, 0)),
            pl.BlockSpec(Y_BLOCK, lambda k: (k, 0, 0, 0, 0)),
            HBM,
        ]
        + [full(x) for x in args],
        out_specs=pl.BlockSpec((64, POOL), lambda k: (0, 0)),
        out_shape=jax.ShapeDtypeStruct((64, POOL), F32),
        scratch_shapes=[
            pltpu.VMEM((POOL, 128), F32),
            pltpu.VMEM((POOL, WIDTH), F32),
            pltpu.VMEM((64, 2, 8, WIDTH), BF16),
        ],
        compiler_params=pltpu.CompilerParams(vmem_limit_bytes=56 << 20),
        cost_estimate=pl.CostEstimate(flops=6 << 30, bytes_accessed=50 << 20, transcendentals=8 << 20),
        name="leaf_b",
    )(u, y, got, *args)


def block_swap(tiles):
    low = iota((8, 128), 1) < 64
    out = [[None] * 8 for _ in range(16)]
    for pair in range(8):
        for g in range(8):
            a, b = tiles[2 * pair][g], tiles[2 * pair + 1][g]
            out[2 * g][pair] = jnp.where(low, a, pltpu.roll(b, 64, 1))
            out[2 * g + 1][pair] = jnp.where(low, pltpu.roll(a, 64, 1), b)
    return out


def own_block(x):
    which = (iota((16, 1024), 1) >> 6) & 3
    out = x[0:16]
    for b in range(1, 4):
        out = jnp.where(which == b, x[b * 16 : (b + 1) * 16], out)
    return out


def dot2(a, b):
    high, low = split(a)
    return dot(high, b) + dot(low, b)


def dot3(a, b):
    high, low = split(b)
    return dot2(a, high) + dot(a.astype(BF16), low)


def finish_kernel(ret_ref, feat_ref, leaf_ref, up2_ref, up1_ref, root_ref, mid_ref, low_ref, out_ref, tile_ref):
    tile_ref[...] = ret_ref[:, 512:640].astype(F32)
    tiles = [[tile_ref[pl.ds(ab * 64 + g, 8, stride=8), :] for g in range(8)] for ab in range(16)]
    swapped = block_swap(tiles)
    s2 = jnp.concatenate([jnp.concatenate(row, axis=1) for row in swapped], axis=0)
    s2 = s2.astype(BF16)
    m2 = dot2(up2_ref[...], s2)
    v = own_block(dot3(up1_ref[...], m2))
    parts = []
    for a in range(4):
        s = v[:, a * 256 : a * 256 + 128] + v[:, a * 256 + 128 : a * 256 + 256]
        s = s + pltpu.roll(s, 64, 1)
        parts.append(jnp.concatenate([s, s], axis=1))
    m1 = jnp.concatenate(parts, axis=0)
    l1 = dot3(root_ref[...], m1)
    l1 = jnp.concatenate([l1[a * 16 : (a + 1) * 16] for a in range(4)], axis=1)
    stack = [l1]
    for shift in range(1, 4):
        stack.append(
            jnp.concatenate(
                [pltpu.roll(m2[:, a * 256 : (a + 1) * 256], 256 - 64 * shift, 1) for a in range(4)], axis=1
            )
        )
    l2 = own_block(dot3(mid_ref[...], jnp.concatenate(stack, axis=0)))
    l3 = dot2(low_ref[:, :128], s2) + dot3(low_ref[:, 128:144], l2)
    swapped = block_swap([[l3[q * 8 : (q + 1) * 8, g * 128 : (g + 1) * 128] for g in range(8)] for q in range(16)])
    l3 = jnp.concatenate([jnp.concatenate(row, axis=1) for row in swapped], axis=0)
    l3_high, l3_low = split(l3)

    n = ROWS
    row = leaf_ref[...]
    col = col_of(row)[:, 0:1]
    same = jnp.where((col == row) & (iota((n, n), 1) < iota((n, n), 0)), 1.0, 0.0).astype(BF16)
    rank = dot(same, jnp.ones((n, 128), BF16))[:, 0:1].astype(jnp.int32)
    slot = col * 8 + rank
    lane = iota((n, 1024), 1)
    near_lo = dot(jnp.where(lane == slot, 1.0, 0.0).astype(BF16), ret_ref[:, :512])
    near_hi = dot(jnp.where(lane == slot + 4, 1.0, 0.0).astype(BF16), ret_ref[:, :512])
    mine = jnp.where(iota((n, 128), 1) == col, 1.0, 0.0).astype(BF16)
    local = dot(mine, l3_high) + dot(mine, l3_low)
    feat = feat_ref[...].astype(F32)
    near = jnp.concatenate([near_lo, near_hi], axis=1)
    out_ref[...] = (feat + near + feat * local).astype(BF16)


def finish(ret, features, leaf_row, mats):
    return pl.pallas_call(
        finish_kernel,
        out_shape=jax.ShapeDtypeStruct((ROWS, WIDTH), BF16),
        scratch_shapes=[pltpu.VMEM((1024, 128), F32)],
        name="finish",
    )(ret, features, leaf_row, *mats)


def blocks(mats, scale, flip):
    m0, m1, m2, m3 = [(m.T if flip else m) * jnp.asarray(scale, m.dtype) for m in mats]
    w1a = jnp.pad(m1, ((0, 64), (0, 64)))
    w1b = jnp.pad(m1, ((64, 0), (64, 0)))
    w2 = jnp.pad(m2, ((0, 128), (0, 128))) + jnp.pad(m2, ((128, 0), (128, 0)))
    w3 = jnp.pad(m3, ((0, 64), (0, 64))) + jnp.pad(m3, ((64, 0), (64, 0)))
    return m0, w1a, w1b, w2, w3


def tree_mats(lift_leaf, lift_branch, couple_root, couple_branch, couple_leaf):
    up2 = lift_leaf.transpose(1, 2, 0).reshape(16, 128)
    up1 = lift_branch.reshape(64, 16)
    keep4 = (1.0 - jnp.eye(4, dtype=F32))[:, :, None, None]
    keep8 = (1.0 - jnp.eye(8, dtype=F32))[:, :, None, None]
    root = (couple_root * keep4).transpose(0, 2, 1, 3).reshape(64, 64)
    mid = [lift_branch.transpose(0, 2, 1).reshape(64, 16)]
    for shift in range(1, 4):
        mid.append(jnp.stack([couple_branch[b, (b + shift) % 4] for b in range(4)]).reshape(64, 16))
    mid = jnp.concatenate(mid, axis=1)
    low = (couple_leaf * keep8).transpose(2, 0, 3, 1).reshape(128, 128)
    lift = lift_leaf.transpose(2, 0, 1).reshape(128, 16)
    return up2, up1, root, mid, jnp.concatenate([low, lift], axis=1)


def degree_table():
    table = np.zeros((256, 128), np.float32)
    for degree in range(4):
        table[degree * 64 : (degree + 1) * 64, degree::4] = 1.0
    return jnp.asarray(table, BF16)


def swap(x):
    return lax.all_to_all(x, AXES, split_axis=0, concat_axis=0, tiled=True)


def shards(
    features,
    cotangent,
    leaf_device,
    neighbours,
    radial,
    first_zero,
    first_one,
    first_two,
    first_three,
    second_zero,
    second_one,
    second_two,
    second_three,
    lift_leaf,
    lift_branch,
    couple_root,
    couple_branch,
    couple_leaf,
):
    leaf_row = leaf_device.reshape(1, ROWS)
    send = pack(leaf_row, features, cotangent)
    got = swap(send.reshape(128, 8, WIDTH))
    rad = jnp.pad(radial.T, ((0, 0), (0, 64)))
    firsts = (first_zero, first_one, first_two, first_three)
    seconds = (second_zero, second_one, second_two, second_three)
    got = got.reshape(64, 2, 8, WIDTH)
    u, y, back, occ = leaf_a(
        got, neighbours, rad, blocks(firsts, 0.5, False), blocks(seconds, 1.0, False)
    )
    ret = swap(back.reshape(128, 8, 640))
    grads = leaf_b(
        u, y, got, occ, blocks(firsts, 0.5, True), blocks(seconds, 1.0, True), degree_table()
    )
    mats = tree_mats(lift_leaf, lift_branch, couple_root, couple_branch, couple_leaf)
    updated = finish(ret.reshape(1024, 640), features, leaf_row, mats)
    return updated, grads


def solution(mesh):
    spread = P(AXES, None)
    across = P(None, AXES)
    return jax.shard_map(
        shards,
        mesh=mesh,
        in_specs=(spread, spread, spread, across, across) + (P(),) * 13,
        out_specs=(spread, across),
        check_vma=False,
    )
```

```python
import math

import jax
import jax.numpy as jnp
import numpy as np
from jax import lax
from jax.experimental import pallas as pl
from jax.experimental.pallas import tpu as pltpu
from jax.sharding import PartitionSpec as P

BF16 = jnp.bfloat16
F32 = jnp.float32
AXES = ("gx", "gy", "gz")
EMPTY = 1024.0
ROWS = 256
POOL = 512
WIDTH = 1024
NBR = 16
TILE = 128


def dot(a, b, **kw):
    return jnp.dot(a, b, preferred_element_type=F32, **kw)


def iota(shape, axis):
    return lax.broadcasted_iota(jnp.int32, shape, axis)


def col_of(row):
    n = row.shape[1]
    diag = jnp.where(iota((n, n), 0) == iota((n, n), 1), row.astype(F32), 0.0).astype(BF16)
    return dot(diag, jnp.ones((n, 128), BF16)).astype(jnp.int32)


def split(x):
    high = x.astype(BF16)
    return high, (x - high.astype(F32)).astype(BF16)


def pack_kernel(leaf_ref, feat_ref, grad_ref, send_ref):
    row = leaf_ref[...]
    col = col_of(row)[:, 0:1]
    n = ROWS
    same = (col == row) & (iota((n, n), 0) < iota((n, n), 1))
    rank = jnp.sum(jnp.where(same, 1.0, 0.0), axis=0, keepdims=True).astype(jnp.int32)
    slot = row * 8 + rank
    ones = jnp.ones((n, 128), BF16)
    for part in range(4):
        index = iota((n, n), 0) + part * n
        pick_f = jnp.where(index == slot, 1.0, 0.0).astype(BF16)
        pick_g = jnp.where(index == slot + 4, 1.0, 0.0).astype(BF16)
        there = dot(pick_f, ones)
        gone = (there < 0.5) & ((iota((n, 128), 0) & 7) < 4)
        out = dot(pick_f, feat_ref[...]) + dot(pick_g, grad_ref[...])
        send_ref[part * n : (part + 1) * n, 128:] = out[:, 128:].astype(BF16)
        send_ref[part * n : (part + 1) * n, :128] = jnp.where(gone, EMPTY, out[:, :128]).astype(BF16)


def pack(leaf_row, features, cotangent):
    return pl.pallas_call(
        pack_kernel,
        out_shape=jax.ShapeDtypeStruct((128 * 8, WIDTH), BF16),
        name="pack",
    )(leaf_row, features, cotangent)


def mix(x, w0, w1a, w1b, w2, w3):
    a = dot(x[:, 0:256], w0)
    b = dot(x[:, 256:512], w1a)
    c = dot(x[:, 384:640], w1b)
    d = dot(x[:, 640:896], w2)
    e = dot(x[:, 896:1024], w3)
    return [
        a[:, :128],
        a[:, 128:],
        b[:, :128],
        b[:, 128:] + c[:, :128],
        c[:, 128:],
        d[:, :128],
        d[:, 128:],
        e,
    ]


def gather(index_ref, pair, part, own_ref, table_ref, out_ref):
    index = [index_ref.at[2 * pair], index_ref.at[2 * pair + 1]]
    for j in range(TILE):
        i = part * TILE + j
        own = own_ref[i * 8 : (i + 1) * 8, :]
        for which in range(2):
            start = pl.multiple_of(index[which][i >> 7, i & 127], 8)
            row = own + table_ref[pl.ds(start, 8), :]
            out_ref[(which * TILE + j) >> 3, pl.ds(j & 7, 8, stride=8), :] = row


def both(a, b):
    return jnp.concatenate([a, b], axis=0)


def scales(rad_ref, rows, pair):
    shifted = pltpu.roll(rad_ref[rows, :], (128 - 8 * pair) % 128, 1)
    r = [jnp.broadcast_to(shifted[:, j : j + 1], (TILE, 128)) for j in range(8)]
    r0, r1, r2, r3 = [both(r[j], r[j + 4]) for j in range(4)]
    low = iota((2 * TILE, 128), 1) < 64
    p01 = jnp.where(low, r0, r1)
    p23 = jnp.where(low, r2, r3)
    p12 = jnp.where(low, r1, r2)
    p31 = jnp.where(low, r3, r1)
    return [p01, p23, p12, p31, p23, p23, p23, r3]


def mix_blocks(piece, w0, w1a, w1b, w2, w3, use, flip=False):
    def times(x, w):
        dims = (((1,), (1 if flip else 0,)), ((), ()))
        return lax.dot_general(x, w[...], dims, preferred_element_type=F32)

    out = times(jnp.concatenate([piece(0), piece(1)], axis=1), w0)
    use(0, out[:, :128])
    use(1, out[:, 128:])
    middle = piece(3)
    a = times(jnp.concatenate([piece(2), middle], axis=1), w1a)
    b = times(jnp.concatenate([middle, piece(4)], axis=1), w1b)
    use(2, a[:, :128])
    use(3, a[:, 128:] + b[:, :128])
    use(4, b[:, 128:])
    out = times(jnp.concatenate([piece(5), piece(6)], axis=1), w2)
    use(5, out[:, :128])
    use(6, out[:, 128:])
    use(7, times(piece(7), w3))


def leaf_a_kernel(
    got_ref,
    nbr_ref,
    rad_ref,
    f0, f1a, f1b, f2, f3,
    s0, s1a, s1b, s2, s3,
    u_ref,
    y_ref,
    back_ref,
    occ_ref,
    own_ref,
    table_ref,
    index_ref,
    acc_ref,
    tile_ref,
    buf0,
    buf1,
    buf2,
    buf3,
    rank_ref,
    rank_smem,
    index_smem,
    sem0,
    sem1,
):
    step = pl.program_id(0)

    @pl.when(step == 0)
    def _():
        first = jnp.where(iota((8, 128), 1) == 0, 1.0, 0.0).astype(BF16)
        got0 = got_ref[:, :, :, 0:128].reshape(1024, 128)
        lead = lax.dot_general(first, got0, (((1,), (1,)), ((), ())), preferred_element_type=F32)
        lane = iota((8, 1024), 1)
        occ = jnp.where((lead < 0.5 * EMPTY) & ((lane & 7) < 4), 1.0, 0.0)
        occ8 = jnp.concatenate([occ[0:1, r * 128 : (r + 1) * 128] for r in range(8)], axis=0)
        occ_ref[...] = occ8
        occ8_low = occ8.astype(BF16)
        before = jnp.where(iota((128, 128), 0) < iota((128, 128), 1), 1.0, 0.0).astype(BF16)
        sums = dot(occ8_low, jnp.ones((128, 128), BF16))
        above = jnp.where(iota((8, 8), 1) < iota((8, 8), 0), 1.0, 0.0).astype(BF16)
        rank = dot(occ8_low, before) + dot(above, sums.astype(BF16))
        filled = jnp.sum(sums, axis=0, keepdims=True)
        rank_ref[...] = 8 * jnp.where(occ8 > 0.5, rank, float(POOL)).astype(jnp.int32)
        to_smem = pltpu.make_async_copy(rank_ref, rank_smem, sem0)
        to_smem.start()
        choice = nbr_ref[...].astype(F32)
        filled = jnp.concatenate([filled] * 4, axis=1)
        left = choice - jnp.floor(choice / filled) * filled
        left = jnp.where(left < 0.0, left + filled, left)
        left = 8 * jnp.where(left >= filled, left - filled, left).astype(jnp.int32)
        for r in range(4):
            index_ref[:, r, :] = left[:, r * 128 : (r + 1) * 128]
        index_to_smem = pltpu.make_async_copy(index_ref, index_smem, sem1)
        index_to_smem.start()
        sums = dot(occ.astype(BF16), got_ref[...].reshape(1024, WIDTH))
        tile_ref[...] = sums * (1.0 / math.sqrt(ROWS))
        for pair in range(64):
            for half in range(2):
                block = got_ref[pair, half].astype(F32)
                at = (pair * 2 + half) * 4
                for g in range(8):
                    own_ref[pl.ds(at * 8 + g, 4, stride=8), :] = block[0:4, g * 128 : (g + 1) * 128]
        acc_ref[...] = jnp.zeros_like(acc_ref)
        to_smem.wait()
        for i in range(POOL):
            s = (i >> 2) * 8 + (i & 3)
            to = pl.multiple_of(rank_smem[s >> 7, s & 127], 8)
            table_ref[pl.ds(to, 8), :] = own_ref[i * 8 : (i + 1) * 8, :]
        index_to_smem.wait()
        gather(index_smem, 0, 0, own_ref, table_ref, buf0)

    bufs = (buf0, buf1, buf2, buf3)
    for turn in range(4):
        after = jnp.minimum(step + (turn + 1) // 4, NBR // 2 - 1)
        gather(index_smem, after, (turn + 1) % 4, own_ref, table_ref, bufs[(turn + 1) % 4])
        rows = pl.ds(turn * TILE, TILE)
        pats = scales(rad_ref, rows, step)

        def piece(g):
            y = bufs[turn][:, g * 8 : (g + 1) * 8, :]
            y_ref[0, turn, :, g * 8 : (g + 1) * 8, :] = y.astype(BF16)
            return (y.reshape(2 * TILE, 128) * pats[g]).astype(BF16)

        def use(g, w):
            cols = slice(g * 128, (g + 1) * 128)
            v = w + w * jnp.tanh(w)
            acc_ref[rows, cols] += v[:TILE] + v[TILE:]
            u_ref[0, rows, cols] = w[:TILE].astype(BF16)
            u_ref[1, rows, cols] = w[TILE:].astype(BF16)

        mix_blocks(piece, f0, f1a, f1b, f2, f3, use)

    @pl.when(step == NBR // 2 - 1)
    def _():
        total = acc_ref[...]
        high, low = split(total)
        wts = (s0[...], s1a[...], s1b[...], s2[...], s3[...])
        near = [0.25 * (a + b) for a, b in zip(mix(high, *wts), mix(low, *wts))]
        half = iota((64, 8, 512), 1) < 4
        lo = jnp.concatenate(near[:4], axis=1)
        hi = jnp.concatenate(near[4:], axis=1)
        lo_r = pltpu.roll(lo.reshape(64, 8, 512), 4, 1)
        hi_r = pltpu.roll(hi.reshape(64, 8, 512), 4, 1)
        lo = lo.reshape(64, 8, 512)
        hi = hi.reshape(64, 8, 512)
        back_ref[:, 0, :, :512] = jnp.where(half, lo, hi_r).astype(BF16)
        back_ref[:, 1, :, :512] = jnp.where(half, lo_r, hi).astype(BF16)
        tile = tile_ref[...]
        body = jnp.concatenate([tile[0:1, r * 128 : (r + 1) * 128] for r in range(8)], axis=0)
        body = jnp.broadcast_to(body[None, None], (64, 2, 8, 128)).astype(BF16)
        back_ref[:, :, :, 512:] = body


def full(x):
    return pl.BlockSpec(x.shape, lambda k, n=len(x.shape): (0,) * n)


WHOLE = pl.BlockSpec(memory_space=pltpu.VMEM)
Y_BLOCK = (1, 4, TILE // 4, 64, 128)


def leaf_a(got, nbr, rad, firsts, seconds):
    args = (nbr, rad, *firsts, *seconds)
    out_shape = [
        jax.ShapeDtypeStruct((NBR, POOL, WIDTH), BF16),
        jax.ShapeDtypeStruct((NBR // 2,) + Y_BLOCK[1:], BF16),
        jax.ShapeDtypeStruct((64, 2, 8, 640), BF16),
        jax.ShapeDtypeStruct((8, 128), F32),
    ]
    return pl.pallas_call(
        leaf_a_kernel,
        grid=(NBR // 2,),
        in_specs=[WHOLE] + [full(x) for x in args],
        out_specs=[
            pl.BlockSpec((2, POOL, WIDTH), lambda k: (k, 0, 0)),
            pl.BlockSpec(Y_BLOCK, lambda k: (k, 0, 0, 0, 0)),
            full(out_shape[2]),
            full(out_shape[3]),
        ],
        out_shape=out_shape,
        scratch_shapes=[
            pltpu.VMEM((POOL * 8, 128), F32),
            pltpu.VMEM((POOL * 8 + 8, 128), F32),
            pltpu.VMEM((NBR, 4, 128), jnp.int32),
            pltpu.VMEM((POOL, WIDTH), F32),
            pltpu.VMEM((8, WIDTH), F32),
        ]
        + [pltpu.VMEM((TILE // 4, 64, 128), F32)] * 4
        + [
            pltpu.VMEM((8, 128), jnp.int32),
            pltpu.SMEM((8, 128), jnp.int32),
            pltpu.SMEM((NBR, 4, 128), jnp.int32),
            pltpu.SemaphoreType.DMA,
            pltpu.SemaphoreType.DMA,
        ],
        compiler_params=pltpu.CompilerParams(vmem_limit_bytes=44 << 20),
        cost_estimate=pl.CostEstimate(flops=6 << 30, bytes_accessed=34 << 20, transcendentals=8 << 20),
        name="leaf_a",
    )(got, *args)


def leaf_b_kernel(
    u_ref, y_ref, got_ref, occ_ref,
    t0, t1a, t1b, t2, t3,
    s0, s1a, s1b, s2, s3,
    sum_ref, out_ref, acc_ref, half_t_ref,
):
    step = pl.program_id(0)

    @pl.when(step == 0)
    def _():
        acc_ref[...] = jnp.zeros_like(acc_ref)
        top = iota((8, WIDTH), 0) < 4
        for part in range(POOL // TILE):
            grad = []
            for pair in range(part * TILE // 8, (part + 1) * TILE // 8):
                a = pltpu.roll(got_ref[pair, 0].astype(F32), 4, 0)
                grad.append(jnp.where(top, a, got_ref[pair, 1].astype(F32)))
            grad = jnp.concatenate(grad, axis=0).astype(BF16)
            rows = slice(part * TILE, (part + 1) * TILE)

            def use(g, value):
                half_t_ref[rows, g * 128 : (g + 1) * 128] = 0.5 * value

            mix_blocks(lambda g: grad[:, g * 128 : (g + 1) * 128], s0, s1a, s1b, s2, s3, use, True)

    for turn in range(4):
        rows = pl.ds(turn * TILE, TILE)
        prods = {}

        def piece(g):
            cols = slice(g * 128, (g + 1) * 128)
            half_t = half_t_ref[rows, cols]
            out = []
            for which in range(2):
                w = u_ref[which, rows, cols].astype(F32)
                h = jnp.tanh(w)
                up = 1.0 + h
                out.append(((up + (w * up) * (1.0 - h)) * half_t).astype(BF16))
            return both(*out)

        def use(g, s):
            y = y_ref[0, turn, :, g * 8 : (g + 1) * 8, :].astype(F32)
            prods[g] = s * y.reshape(2 * TILE, 128)

        mix_blocks(piece, t0, t1a, t1b, t2, t3, use)
        low = iota((2 * TILE, 128), 1) < 64
        ones = jnp.where(low, prods[2], prods[3])
        ones = ones + pltpu.roll(ones, 64, 1)
        threes = prods[7] + pltpu.roll(prods[7], 64, 1)
        cross = pltpu.roll(jnp.where(low, prods[3], prods[2]), 64, 1)
        x01 = prods[0] + jnp.where(low, 0.0, ones)
        x23 = (prods[1] + prods[4]) + (prods[5] + prods[6]) + cross + jnp.where(low, 0.0, threes)
        sums = dot(jnp.concatenate([x01, x23], axis=1).astype(BF16), sum_ref[...])
        owner = iota((TILE, 128), 1) >> 2
        kept = jnp.where(owner == 2 * step, sums[:TILE], acc_ref[rows, :])
        acc_ref[rows, :] = jnp.where(owner == 2 * step + 1, sums[TILE:], kept)

    @pl.when(step == NBR // 2 - 1)
    def _():
        occ = []
        for r in range(8):
            pick = iota((128, 64), 0) == (iota((128, 64), 1) >> 2) * 8 + (iota((128, 64), 1) & 3)
            occ.append(dot(occ_ref[r : r + 1, :].astype(BF16), jnp.where(pick, 1.0, 0.0).astype(BF16)))
        occ = jnp.concatenate(occ, axis=1)
        out_ref[...] = 0.5 * occ * jnp.transpose(acc_ref[...])[0:64, :]


def leaf_b(u, y, got, occ, firsts_t, seconds, sums):
    args = (occ, *firsts_t, *seconds, sums)
    return pl.pallas_call(
        leaf_b_kernel,
        grid=(NBR // 2,),
        in_specs=[
            pl.BlockSpec((2, POOL, WIDTH), lambda k: (k, 0, 0)),
            pl.BlockSpec(Y_BLOCK, lambda k: (k, 0, 0, 0, 0)),
            WHOLE,
        ]
        + [full(x) for x in args],
        out_specs=pl.BlockSpec((64, POOL), lambda k: (0, 0)),
        out_shape=jax.ShapeDtypeStruct((64, POOL), F32),
        scratch_shapes=[
            pltpu.VMEM((POOL, 128), F32),
            pltpu.VMEM((POOL, WIDTH), F32),
        ],
        compiler_params=pltpu.CompilerParams(vmem_limit_bytes=44 << 20),
        cost_estimate=pl.CostEstimate(flops=6 << 30, bytes_accessed=34 << 20, transcendentals=8 << 20),
        name="leaf_b",
    )(u, y, got, *args)


def block_swap(tiles):
    low = iota((8, 128), 1) < 64
    out = [[None] * 8 for _ in range(16)]
    for pair in range(8):
        for g in range(8):
            a, b = tiles[2 * pair][g], tiles[2 * pair + 1][g]
            out[2 * g][pair] = jnp.where(low, a, pltpu.roll(b, 64, 1))
            out[2 * g + 1][pair] = jnp.where(low, pltpu.roll(a, 64, 1), b)
    return out


def own_block(x):
    which = (iota((16, 1024), 1) >> 6) & 3
    out = x[0:16]
    for b in range(1, 4):
        out = jnp.where(which == b, x[b * 16 : (b + 1) * 16], out)
    return out


def dot2(a, b):
    high, low = split(a)
    return dot(high, b) + dot(low, b)


def dot3(a, b):
    high, low = split(b)
    return dot2(a, high) + dot(a.astype(BF16), low)


def finish_kernel(ret_ref, feat_ref, leaf_ref, up2_ref, up1_ref, root_ref, mid_ref, low_ref, out_ref, tile_ref):
    tile_ref[...] = ret_ref[:, 512:640].astype(F32)
    tiles = [[tile_ref[pl.ds(ab * 64 + g, 8, stride=8), :] for g in range(8)] for ab in range(16)]
    swapped = block_swap(tiles)
    s2 = jnp.concatenate([jnp.concatenate(row, axis=1) for row in swapped], axis=0)
    s2 = s2.astype(BF16)
    m2 = dot2(up2_ref[...], s2)
    v = own_block(dot3(up1_ref[...], m2))
    parts = []
    for a in range(4):
        s = v[:, a * 256 : a * 256 + 128] + v[:, a * 256 + 128 : a * 256 + 256]
        s = s + pltpu.roll(s, 64, 1)
        parts.append(jnp.concatenate([s, s], axis=1))
    m1 = jnp.concatenate(parts, axis=0)
    l1 = dot3(root_ref[...], m1)
    l1 = jnp.concatenate([l1[a * 16 : (a + 1) * 16] for a in range(4)], axis=1)
    stack = [l1]
    for shift in range(1, 4):
        stack.append(
            jnp.concatenate(
                [pltpu.roll(m2[:, a * 256 : (a + 1) * 256], 256 - 64 * shift, 1) for a in range(4)], axis=1
            )
        )
    l2 = own_block(dot3(mid_ref[...], jnp.concatenate(stack, axis=0)))
    l3 = dot2(low_ref[:, :128], s2) + dot3(low_ref[:, 128:144], l2)
    swapped = block_swap([[l3[q * 8 : (q + 1) * 8, g * 128 : (g + 1) * 128] for g in range(8)] for q in range(16)])
    l3 = jnp.concatenate([jnp.concatenate(row, axis=1) for row in swapped], axis=0)
    l3_high, l3_low = split(l3)

    n = ROWS
    row = leaf_ref[...]
    col = col_of(row)[:, 0:1]
    same = jnp.where((col == row) & (iota((n, n), 1) < iota((n, n), 0)), 1.0, 0.0).astype(BF16)
    rank = dot(same, jnp.ones((n, 128), BF16))[:, 0:1].astype(jnp.int32)
    slot = col * 8 + rank
    lane = iota((n, 1024), 1)
    near_lo = dot(jnp.where(lane == slot, 1.0, 0.0).astype(BF16), ret_ref[:, :512])
    near_hi = dot(jnp.where(lane == slot + 4, 1.0, 0.0).astype(BF16), ret_ref[:, :512])
    mine = jnp.where(iota((n, 128), 1) == col, 1.0, 0.0).astype(BF16)
    local = dot(mine, l3_high) + dot(mine, l3_low)
    feat = feat_ref[...].astype(F32)
    near = jnp.concatenate([near_lo, near_hi], axis=1)
    out_ref[...] = (feat + near + feat * local).astype(BF16)


def finish(ret, features, leaf_row, mats):
    return pl.pallas_call(
        finish_kernel,
        out_shape=jax.ShapeDtypeStruct((ROWS, WIDTH), BF16),
        scratch_shapes=[pltpu.VMEM((1024, 128), F32)],
        name="finish",
    )(ret, features, leaf_row, *mats)


def blocks(mats, scale, flip):
    m0, m1, m2, m3 = [(m.T if flip else m) * jnp.asarray(scale, m.dtype) for m in mats]
    w1a = jnp.pad(m1, ((0, 64), (0, 64)))
    w1b = jnp.pad(m1, ((64, 0), (64, 0)))
    w2 = jnp.pad(m2, ((0, 128), (0, 128))) + jnp.pad(m2, ((128, 0), (128, 0)))
    w3 = jnp.pad(m3, ((0, 64), (0, 64))) + jnp.pad(m3, ((64, 0), (64, 0)))
    return m0, w1a, w1b, w2, w3


def tree_mats(lift_leaf, lift_branch, couple_root, couple_branch, couple_leaf):
    up2 = lift_leaf.transpose(1, 2, 0).reshape(16, 128)
    up1 = lift_branch.reshape(64, 16)
    keep4 = (1.0 - jnp.eye(4, dtype=F32))[:, :, None, None]
    keep8 = (1.0 - jnp.eye(8, dtype=F32))[:, :, None, None]
    root = (couple_root * keep4).transpose(0, 2, 1, 3).reshape(64, 64)
    mid = [lift_branch.transpose(0, 2, 1).reshape(64, 16)]
    for shift in range(1, 4):
        mid.append(jnp.stack([couple_branch[b, (b + shift) % 4] for b in range(4)]).reshape(64, 16))
    mid = jnp.concatenate(mid, axis=1)
    low = (couple_leaf * keep8).transpose(2, 0, 3, 1).reshape(128, 128)
    lift = lift_leaf.transpose(2, 0, 1).reshape(128, 16)
    return up2, up1, root, mid, jnp.concatenate([low, lift], axis=1)


def degree_table():
    table = np.zeros((256, 128), np.float32)
    for degree in range(4):
        table[degree * 64 : (degree + 1) * 64, degree::4] = 1.0
    return jnp.asarray(table, BF16)


def swap(x):
    return lax.all_to_all(x, AXES, split_axis=0, concat_axis=0, tiled=True)


def shards(
    features,
    cotangent,
    leaf_device,
    neighbours,
    radial,
    first_zero,
    first_one,
    first_two,
    first_three,
    second_zero,
    second_one,
    second_two,
    second_three,
    lift_leaf,
    lift_branch,
    couple_root,
    couple_branch,
    couple_leaf,
):
    leaf_row = leaf_device.reshape(1, ROWS)
    send = pack(leaf_row, features, cotangent)
    got = swap(send.reshape(128, 8, WIDTH))
    rad = jnp.pad(radial.T, ((0, 0), (0, 64)))
    firsts = (first_zero, first_one, first_two, first_three)
    seconds = (second_zero, second_one, second_two, second_three)
    got = got.reshape(64, 2, 8, WIDTH)
    firsts_t = blocks(firsts, 0.5, True)
    seconds = blocks(seconds, 1.0, False)
    mats = tree_mats(lift_leaf, lift_branch, couple_root, couple_branch, couple_leaf)
    got, firsts_t, mats = lax.optimization_barrier((got, firsts_t, mats))
    u, y, back, occ = leaf_a(got, neighbours, rad, blocks(firsts, 0.5, False), seconds)
    ret = swap(back.reshape(128, 8, 640))
    grads = leaf_b(u, y, got, occ, firsts_t, seconds, degree_table())
    updated = finish(ret.reshape(1024, 640), features, leaf_row, mats)
    return updated, grads


def solution(mesh):
    spread = P(AXES, None)
    across = P(None, AXES)
    return jax.shard_map(
        shards,
        mesh=mesh,
        in_specs=(spread, spread, spread, across, across) + (P(),) * 13,
        out_specs=(spread, across),
        check_vma=False,
    )
```

```python
import math

import jax
import jax.numpy as jnp
import numpy as np
from jax import lax
from jax.experimental import pallas as pl
from jax.experimental.pallas import tpu as pltpu
from jax.sharding import PartitionSpec as P

BF16 = jnp.bfloat16
F32 = jnp.float32
AXES = ("gx", "gy", "gz")
EMPTY = 1024.0
ROWS = 256
POOL = 512
WIDTH = 1024
NBR = 16
TILE = 128


def dot(a, b, **kw):
    return jnp.dot(a, b, preferred_element_type=F32, **kw)


def iota(shape, axis):
    return lax.broadcasted_iota(jnp.int32, shape, axis)


def col_of(row):
    n = row.shape[1]
    diag = jnp.where(iota((n, n), 0) == iota((n, n), 1), row.astype(F32), 0.0).astype(BF16)
    return dot(diag, jnp.ones((n, 128), BF16)).astype(jnp.int32)


def split(x):
    high = x.astype(BF16)
    return high, (x - high.astype(F32)).astype(BF16)


def pack_kernel(leaf_ref, feat_ref, grad_ref, send_ref, slot_ref):
    part = pl.program_id(0)
    n = ROWS

    @pl.when(part == 0)
    def _():
        row = leaf_ref[...]
        col = col_of(row)[:, 0:1]
        same = (col == row) & (iota((n, n), 0) < iota((n, n), 1))
        rank = jnp.sum(jnp.where(same, 1.0, 0.0), axis=0, keepdims=True).astype(jnp.int32)
        slot_ref[...] = jnp.broadcast_to(row * 8 + rank, (8, n))

    slot = slot_ref[0:1, :]
    index = iota((n, n), 0) + part * n
    pick_f = jnp.where(index == slot, 1.0, 0.0).astype(BF16)
    pick_g = jnp.where(index == slot + 4, 1.0, 0.0).astype(BF16)
    there = dot(pick_f, jnp.ones((n, 128), BF16))
    gone = (there < 0.5) & ((iota((n, 128), 0) & 7) < 4)
    out = dot(pick_f, feat_ref[...]) + dot(pick_g, grad_ref[...])
    send_ref[:, 128:] = out[:, 128:].astype(BF16)
    send_ref[:, :128] = jnp.where(gone, EMPTY, out[:, :128]).astype(BF16)


def pack(leaf_row, features, cotangent):
    args = (leaf_row, features, cotangent)
    return pl.pallas_call(
        pack_kernel,
        grid=(4,),
        in_specs=[full(x) for x in args],
        out_specs=pl.BlockSpec((ROWS, WIDTH), lambda k: (k, 0)),
        out_shape=jax.ShapeDtypeStruct((128 * 8, WIDTH), BF16),
        scratch_shapes=[pltpu.VMEM((8, ROWS), jnp.int32)],
        name="pack",
    )(*args)


def mix(x, w0, w1a, w1b, w2, w3):
    a = dot(x[:, 0:256], w0)
    b = dot(x[:, 256:512], w1a)
    c = dot(x[:, 384:640], w1b)
    d = dot(x[:, 640:896], w2)
    e = dot(x[:, 896:1024], w3)
    return [
        a[:, :128],
        a[:, 128:],
        b[:, :128],
        b[:, 128:] + c[:, :128],
        c[:, 128:],
        d[:, :128],
        d[:, 128:],
        e,
    ]


def gather(index_ref, pair, part, own_ref, table_ref, out_ref):
    index = [index_ref.at[2 * pair], index_ref.at[2 * pair + 1]]
    for j in range(TILE):
        i = part * TILE + j
        own = own_ref[i * 8 : (i + 1) * 8, :]
        for which in range(2):
            start = pl.multiple_of(index[which][i >> 7, i & 127], 8)
            row = own + table_ref[pl.ds(start, 8), :]
            out_ref[(which * TILE + j) >> 3, pl.ds(j & 7, 8, stride=8), :] = row


def both(a, b):
    return jnp.concatenate([a, b], axis=0)


def scales(rad_ref, rows, pair):
    shifted = pltpu.roll(rad_ref[rows, :], (128 - 8 * pair) % 128, 1)
    r = [jnp.broadcast_to(shifted[:, j : j + 1], (TILE, 128)) for j in range(8)]
    r0, r1, r2, r3 = [both(r[j], r[j + 4]) for j in range(4)]
    low = iota((2 * TILE, 128), 1) < 64
    p01 = jnp.where(low, r0, r1)
    p23 = jnp.where(low, r2, r3)
    p12 = jnp.where(low, r1, r2)
    p31 = jnp.where(low, r3, r1)
    return [p01, p23, p12, p31, p23, p23, p23, r3]


def mix_blocks(piece, w0, w1a, w1b, w2, w3, use, flip=False):
    def times(x, w):
        dims = (((1,), (1 if flip else 0,)), ((), ()))
        return lax.dot_general(x, w[...], dims, preferred_element_type=F32)

    out = times(jnp.concatenate([piece(0), piece(1)], axis=1), w0)
    use(0, out[:, :128])
    use(1, out[:, 128:])
    middle = piece(3)
    a = times(jnp.concatenate([piece(2), middle], axis=1), w1a)
    b = times(jnp.concatenate([middle, piece(4)], axis=1), w1b)
    use(2, a[:, :128])
    use(3, a[:, 128:] + b[:, :128])
    use(4, b[:, 128:])
    out = times(jnp.concatenate([piece(5), piece(6)], axis=1), w2)
    use(5, out[:, :128])
    use(6, out[:, 128:])
    use(7, times(piece(7), w3))


def leaf_a_kernel(
    got_ref,
    nbr_ref,
    rad_ref,
    f0_hbm, f1a_hbm, f1b_hbm, f2_hbm, f3_hbm,
    s0, s1a, s1b, s2, s3,
    u_ref,
    y_ref,
    back_ref,
    occ_ref,
    own_ref,
    table_ref,
    index_ref,
    acc_ref,
    tile_ref,
    buf0,
    buf1,
    buf2,
    buf3,
    rank_ref,
    rank_smem,
    index_smem,
    f0, f1a, f1b, f2, f3,
    sem0,
    sem1,
    sems,
):
    step = pl.program_id(0)
    pairs = ((f0_hbm, f0), (f1a_hbm, f1a), (f1b_hbm, f1b), (f2_hbm, f2), (f3_hbm, f3))
    weights = [pltpu.make_async_copy(a, b, sems.at[i]) for i, (a, b) in enumerate(pairs)]

    @pl.when(step == 0)
    def _():
        for copy in weights:
            copy.start()
        first = jnp.where(iota((8, 128), 1) == 0, 1.0, 0.0).astype(BF16)
        got0 = got_ref[:, :, :, 0:128].reshape(1024, 128)
        lead = lax.dot_general(first, got0, (((1,), (1,)), ((), ())), preferred_element_type=F32)
        lane = iota((8, 1024), 1)
        occ = jnp.where((lead < 0.5 * EMPTY) & ((lane & 7) < 4), 1.0, 0.0)
        occ8 = jnp.concatenate([occ[0:1, r * 128 : (r + 1) * 128] for r in range(8)], axis=0)
        occ_ref[...] = occ8
        occ8_low = occ8.astype(BF16)
        before = jnp.where(iota((128, 128), 0) < iota((128, 128), 1), 1.0, 0.0).astype(BF16)
        sums = dot(occ8_low, jnp.ones((128, 128), BF16))
        above = jnp.where(iota((8, 8), 1) < iota((8, 8), 0), 1.0, 0.0).astype(BF16)
        rank = dot(occ8_low, before) + dot(above, sums.astype(BF16))
        filled = jnp.sum(sums, axis=0, keepdims=True)
        rank_ref[...] = 8 * jnp.where(occ8 > 0.5, rank, float(POOL)).astype(jnp.int32)
        to_smem = pltpu.make_async_copy(rank_ref, rank_smem, sem0)
        to_smem.start()
        choice = nbr_ref[...].astype(F32)
        filled = jnp.concatenate([filled] * 4, axis=1)
        left = choice - jnp.floor(choice / filled) * filled
        left = jnp.where(left < 0.0, left + filled, left)
        left = 8 * jnp.where(left >= filled, left - filled, left).astype(jnp.int32)
        for r in range(4):
            index_ref[:, r, :] = left[:, r * 128 : (r + 1) * 128]
        index_to_smem = pltpu.make_async_copy(index_ref, index_smem, sem1)
        index_to_smem.start()
        sums = dot(occ.astype(BF16), got_ref[...].reshape(1024, WIDTH))
        tile_ref[...] = sums * (1.0 / math.sqrt(ROWS))
        for pair in range(64):
            for half in range(2):
                block = got_ref[pair, half].astype(F32)
                at = (pair * 2 + half) * 4
                for g in range(8):
                    own_ref[pl.ds(at * 8 + g, 4, stride=8), :] = block[0:4, g * 128 : (g + 1) * 128]
        acc_ref[...] = jnp.zeros_like(acc_ref)
        to_smem.wait()
        for i in range(POOL):
            s = (i >> 2) * 8 + (i & 3)
            to = pl.multiple_of(rank_smem[s >> 7, s & 127], 8)
            table_ref[pl.ds(to, 8), :] = own_ref[i * 8 : (i + 1) * 8, :]
        index_to_smem.wait()
        gather(index_smem, 0, 0, own_ref, table_ref, buf0)
        for copy in weights:
            copy.wait()

    bufs = (buf0, buf1, buf2, buf3)
    for turn in range(4):
        after = jnp.minimum(step + (turn + 1) // 4, NBR // 2 - 1)
        gather(index_smem, after, (turn + 1) % 4, own_ref, table_ref, bufs[(turn + 1) % 4])
        rows = pl.ds(turn * TILE, TILE)
        pats = scales(rad_ref, rows, step)

        def piece(g):
            y = bufs[turn][:, g * 8 : (g + 1) * 8, :]
            y_ref[0, turn, :, g * 8 : (g + 1) * 8, :] = y.astype(BF16)
            return (y.reshape(2 * TILE, 128) * pats[g]).astype(BF16)

        def use(g, w):
            cols = slice(g * 128, (g + 1) * 128)
            v = w + w * jnp.tanh(w)
            acc_ref[rows, cols] += v[:TILE] + v[TILE:]
            u_ref[0, rows, cols] = w[:TILE].astype(BF16)
            u_ref[1, rows, cols] = w[TILE:].astype(BF16)

        mix_blocks(piece, f0, f1a, f1b, f2, f3, use)

    @pl.when(step == NBR // 2 - 1)
    def _():
        total = acc_ref[...]
        high, low = split(total)
        wts = (s0[...], s1a[...], s1b[...], s2[...], s3[...])
        near = [0.25 * (a + b) for a, b in zip(mix(high, *wts), mix(low, *wts))]
        half = iota((64, 8, 512), 1) < 4
        lo = jnp.concatenate(near[:4], axis=1)
        hi = jnp.concatenate(near[4:], axis=1)
        lo_r = pltpu.roll(lo.reshape(64, 8, 512), 4, 1)
        hi_r = pltpu.roll(hi.reshape(64, 8, 512), 4, 1)
        lo = lo.reshape(64, 8, 512)
        hi = hi.reshape(64, 8, 512)
        back_ref[:, 0, :, :512] = jnp.where(half, lo, hi_r).astype(BF16)
        back_ref[:, 1, :, :512] = jnp.where(half, lo_r, hi).astype(BF16)
        tile = tile_ref[...]
        body = jnp.concatenate([tile[0:1, r * 128 : (r + 1) * 128] for r in range(8)], axis=0)
        body = jnp.broadcast_to(body[None, None], (64, 2, 8, 128)).astype(BF16)
        back_ref[:, :, :, 512:] = body


def full(x):
    return pl.BlockSpec(x.shape, lambda k, n=len(x.shape): (0,) * n)


WHOLE = pl.BlockSpec(memory_space=pltpu.VMEM)
HBM = pl.BlockSpec(memory_space=pltpu.HBM)
Y_BLOCK = (1, 4, TILE // 4, 64, 128)


def leaf_a(got, nbr, rad, firsts, seconds):
    out_shape = [
        jax.ShapeDtypeStruct((NBR, POOL, WIDTH), BF16),
        jax.ShapeDtypeStruct((NBR // 2,) + Y_BLOCK[1:], BF16),
        jax.ShapeDtypeStruct((64, 2, 8, 640), BF16),
        jax.ShapeDtypeStruct((8, 128), F32),
    ]
    return pl.pallas_call(
        leaf_a_kernel,
        grid=(NBR // 2,),
        in_specs=[WHOLE, full(nbr), full(rad)] + [HBM] * 5 + [full(x) for x in seconds],
        out_specs=[
            pl.BlockSpec((2, POOL, WIDTH), lambda k: (k, 0, 0)),
            pl.BlockSpec(Y_BLOCK, lambda k: (k, 0, 0, 0, 0)),
            full(out_shape[2]),
            full(out_shape[3]),
        ],
        out_shape=out_shape,
        scratch_shapes=[
            pltpu.VMEM((POOL * 8, 128), F32),
            pltpu.VMEM((POOL * 8 + 8, 128), F32),
            pltpu.VMEM((NBR, 4, 128), jnp.int32),
            pltpu.VMEM((POOL, WIDTH), F32),
            pltpu.VMEM((8, WIDTH), F32),
        ]
        + [pltpu.VMEM((TILE // 4, 64, 128), F32)] * 4
        + [
            pltpu.VMEM((8, 128), jnp.int32),
            pltpu.SMEM((8, 128), jnp.int32),
            pltpu.SMEM((NBR, 4, 128), jnp.int32),
        ]
        + [pltpu.VMEM(x.shape, BF16) for x in firsts]
        + [
            pltpu.SemaphoreType.DMA,
            pltpu.SemaphoreType.DMA,
            pltpu.SemaphoreType.DMA((5,)),
        ],
        compiler_params=pltpu.CompilerParams(vmem_limit_bytes=60 << 20),
        cost_estimate=pl.CostEstimate(flops=6 << 30, bytes_accessed=34 << 20, transcendentals=8 << 20),
        name="leaf_a",
    )(got, nbr, rad, *firsts, *seconds)


def leaf_b_kernel(
    u_ref, y_ref, got_ref, occ_ref,
    t0, t1a, t1b, t2, t3,
    s0, s1a, s1b, s2, s3,
    sum_ref, out_ref, acc_ref, half_t_ref,
):
    step = pl.program_id(0)

    @pl.when(step == 0)
    def _():
        acc_ref[...] = jnp.zeros_like(acc_ref)
        top = iota((8, WIDTH), 0) < 4
        for part in range(POOL // TILE):
            grad = []
            for pair in range(part * TILE // 8, (part + 1) * TILE // 8):
                a = pltpu.roll(got_ref[pair, 0].astype(F32), 4, 0)
                grad.append(jnp.where(top, a, got_ref[pair, 1].astype(F32)))
            grad = jnp.concatenate(grad, axis=0).astype(BF16)
            rows = slice(part * TILE, (part + 1) * TILE)

            def use(g, value):
                half_t_ref[rows, g * 128 : (g + 1) * 128] = 0.5 * value

            mix_blocks(lambda g: grad[:, g * 128 : (g + 1) * 128], s0, s1a, s1b, s2, s3, use, True)

    for turn in range(4):
        rows = pl.ds(turn * TILE, TILE)
        prods = {}

        def piece(g):
            cols = slice(g * 128, (g + 1) * 128)
            half_t = half_t_ref[rows, cols]
            out = []
            for which in range(2):
                w = u_ref[which, rows, cols].astype(F32)
                h = jnp.tanh(w)
                up = 1.0 + h
                out.append(((up + (w * up) * (1.0 - h)) * half_t).astype(BF16))
            return both(*out)

        def use(g, s):
            y = y_ref[0, turn, :, g * 8 : (g + 1) * 8, :].astype(F32)
            prods[g] = s * y.reshape(2 * TILE, 128)

        mix_blocks(piece, t0, t1a, t1b, t2, t3, use)
        low = iota((2 * TILE, 128), 1) < 64
        ones = jnp.where(low, prods[2], prods[3])
        ones = ones + pltpu.roll(ones, 64, 1)
        threes = prods[7] + pltpu.roll(prods[7], 64, 1)
        cross = pltpu.roll(jnp.where(low, prods[3], prods[2]), 64, 1)
        x01 = prods[0] + jnp.where(low, 0.0, ones)
        x23 = (prods[1] + prods[4]) + (prods[5] + prods[6]) + cross + jnp.where(low, 0.0, threes)
        sums = dot(jnp.concatenate([x01, x23], axis=1).astype(BF16), sum_ref[...])
        owner = iota((TILE, 128), 1) >> 2
        kept = jnp.where(owner == 2 * step, sums[:TILE], acc_ref[rows, :])
        acc_ref[rows, :] = jnp.where(owner == 2 * step + 1, sums[TILE:], kept)

    @pl.when(step == NBR // 2 - 1)
    def _():
        occ = []
        for r in range(8):
            pick = iota((128, 64), 0) == (iota((128, 64), 1) >> 2) * 8 + (iota((128, 64), 1) & 3)
            occ.append(dot(occ_ref[r : r + 1, :].astype(BF16), jnp.where(pick, 1.0, 0.0).astype(BF16)))
        occ = jnp.concatenate(occ, axis=1)
        out_ref[...] = 0.5 * occ * jnp.transpose(acc_ref[...])[0:64, :]


def leaf_b(u, y, got, occ, firsts_t, seconds, sums):
    args = (occ, *firsts_t, *seconds, sums)
    return pl.pallas_call(
        leaf_b_kernel,
        grid=(NBR // 2,),
        in_specs=[
            pl.BlockSpec((2, POOL, WIDTH), lambda k: (k, 0, 0)),
            pl.BlockSpec(Y_BLOCK, lambda k: (k, 0, 0, 0, 0)),
            WHOLE,
        ]
        + [full(x) for x in args],
        out_specs=pl.BlockSpec((64, POOL), lambda k: (0, 0)),
        out_shape=jax.ShapeDtypeStruct((64, POOL), F32),
        scratch_shapes=[
            pltpu.VMEM((POOL, 128), F32),
            pltpu.VMEM((POOL, WIDTH), F32),
        ],
        compiler_params=pltpu.CompilerParams(vmem_limit_bytes=44 << 20),
        cost_estimate=pl.CostEstimate(flops=6 << 30, bytes_accessed=34 << 20, transcendentals=8 << 20),
        name="leaf_b",
    )(u, y, got, *args)


def block_swap(tiles):
    low = iota((8, 128), 1) < 64
    out = [[None] * 8 for _ in range(16)]
    for pair in range(8):
        for g in range(8):
            a, b = tiles[2 * pair][g], tiles[2 * pair + 1][g]
            out[2 * g][pair] = jnp.where(low, a, pltpu.roll(b, 64, 1))
            out[2 * g + 1][pair] = jnp.where(low, pltpu.roll(a, 64, 1), b)
    return out


def own_block(x):
    which = (iota((16, 1024), 1) >> 6) & 3
    out = x[0:16]
    for b in range(1, 4):
        out = jnp.where(which == b, x[b * 16 : (b + 1) * 16], out)
    return out


def dot2(a, b):
    high, low = split(a)
    return dot(high, b) + dot(low, b)


def dot3(a, b):
    high, low = split(b)
    return dot2(a, high) + dot(a.astype(BF16), low)


def finish_kernel(ret_ref, feat_ref, leaf_ref, up2_ref, up1_ref, root_ref, mid_ref, low_ref, out_ref, tile_ref):
    tile_ref[...] = ret_ref[:, 512:640].astype(F32)
    tiles = [[tile_ref[pl.ds(ab * 64 + g, 8, stride=8), :] for g in range(8)] for ab in range(16)]
    swapped = block_swap(tiles)
    s2 = jnp.concatenate([jnp.concatenate(row, axis=1) for row in swapped], axis=0)
    s2 = s2.astype(BF16)
    m2 = dot2(up2_ref[...], s2)
    v = own_block(dot3(up1_ref[...], m2))
    parts = []
    for a in range(4):
        s = v[:, a * 256 : a * 256 + 128] + v[:, a * 256 + 128 : a * 256 + 256]
        s = s + pltpu.roll(s, 64, 1)
        parts.append(jnp.concatenate([s, s], axis=1))
    m1 = jnp.concatenate(parts, axis=0)
    l1 = dot3(root_ref[...], m1)
    l1 = jnp.concatenate([l1[a * 16 : (a + 1) * 16] for a in range(4)], axis=1)
    stack = [l1]
    for shift in range(1, 4):
        stack.append(
            jnp.concatenate(
                [pltpu.roll(m2[:, a * 256 : (a + 1) * 256], 256 - 64 * shift, 1) for a in range(4)], axis=1
            )
        )
    l2 = own_block(dot3(mid_ref[...], jnp.concatenate(stack, axis=0)))
    l3 = dot2(low_ref[:, :128], s2) + dot3(low_ref[:, 128:144], l2)
    swapped = block_swap([[l3[q * 8 : (q + 1) * 8, g * 128 : (g + 1) * 128] for g in range(8)] for q in range(16)])
    l3 = jnp.concatenate([jnp.concatenate(row, axis=1) for row in swapped], axis=0)
    l3_high, l3_low = split(l3)

    n = ROWS
    row = leaf_ref[...]
    col = col_of(row)[:, 0:1]
    same = jnp.where((col == row) & (iota((n, n), 1) < iota((n, n), 0)), 1.0, 0.0).astype(BF16)
    rank = dot(same, jnp.ones((n, 128), BF16))[:, 0:1].astype(jnp.int32)
    slot = col * 8 + rank
    lane = iota((n, 1024), 1)
    near_lo = dot(jnp.where(lane == slot, 1.0, 0.0).astype(BF16), ret_ref[:, :512])
    near_hi = dot(jnp.where(lane == slot + 4, 1.0, 0.0).astype(BF16), ret_ref[:, :512])
    mine = jnp.where(iota((n, 128), 1) == col, 1.0, 0.0).astype(BF16)
    local = dot(mine, l3_high) + dot(mine, l3_low)
    feat = feat_ref[...].astype(F32)
    near = jnp.concatenate([near_lo, near_hi], axis=1)
    out_ref[...] = (feat + near + feat * local).astype(BF16)


def finish(ret, features, leaf_row, mats):
    return pl.pallas_call(
        finish_kernel,
        out_shape=jax.ShapeDtypeStruct((ROWS, WIDTH), BF16),
        scratch_shapes=[pltpu.VMEM((1024, 128), F32)],
        name="finish",
    )(ret, features, leaf_row, *mats)


def blocks(mats, scale, flip):
    m0, m1, m2, m3 = [(m.T if flip else m) * jnp.asarray(scale, m.dtype) for m in mats]
    w1a = jnp.pad(m1, ((0, 64), (0, 64)))
    w1b = jnp.pad(m1, ((64, 0), (64, 0)))
    w2 = jnp.pad(m2, ((0, 128), (0, 128))) + jnp.pad(m2, ((128, 0), (128, 0)))
    w3 = jnp.pad(m3, ((0, 64), (0, 64))) + jnp.pad(m3, ((64, 0), (64, 0)))
    return m0, w1a, w1b, w2, w3


def tree_mats(lift_leaf, lift_branch, couple_root, couple_branch, couple_leaf):
    up2 = lift_leaf.transpose(1, 2, 0).reshape(16, 128)
    up1 = lift_branch.reshape(64, 16)
    keep4 = (1.0 - jnp.eye(4, dtype=F32))[:, :, None, None]
    keep8 = (1.0 - jnp.eye(8, dtype=F32))[:, :, None, None]
    root = (couple_root * keep4).transpose(0, 2, 1, 3).reshape(64, 64)
    mid = [lift_branch.transpose(0, 2, 1).reshape(64, 16)]
    for shift in range(1, 4):
        mid.append(jnp.stack([couple_branch[b, (b + shift) % 4] for b in range(4)]).reshape(64, 16))
    mid = jnp.concatenate(mid, axis=1)
    low = (couple_leaf * keep8).transpose(2, 0, 3, 1).reshape(128, 128)
    lift = lift_leaf.transpose(2, 0, 1).reshape(128, 16)
    return up2, up1, root, mid, jnp.concatenate([low, lift], axis=1)


def degree_table():
    table = np.zeros((256, 128), np.float32)
    for degree in range(4):
        table[degree * 64 : (degree + 1) * 64, degree::4] = 1.0
    return jnp.asarray(table, BF16)


def swap(x):
    return lax.all_to_all(x, AXES, split_axis=0, concat_axis=0, tiled=True)


def shards(
    features,
    cotangent,
    leaf_device,
    neighbours,
    radial,
    first_zero,
    first_one,
    first_two,
    first_three,
    second_zero,
    second_one,
    second_two,
    second_three,
    lift_leaf,
    lift_branch,
    couple_root,
    couple_branch,
    couple_leaf,
):
    leaf_row = leaf_device.reshape(1, ROWS)
    send = pack(leaf_row, features, cotangent)
    got = swap(send.reshape(128, 8, WIDTH))
    rad = jnp.pad(radial.T, ((0, 0), (0, 64)))
    firsts = (first_zero, first_one, first_two, first_three)
    seconds = (second_zero, second_one, second_two, second_three)
    got = got.reshape(64, 2, 8, WIDTH)
    firsts_t = blocks(firsts, 0.5, True)
    seconds = blocks(seconds, 1.0, False)
    mats = tree_mats(lift_leaf, lift_branch, couple_root, couple_branch, couple_leaf)
    got, firsts_t, mats = lax.optimization_barrier((got, firsts_t, mats))
    u, y, back, occ = leaf_a(got, neighbours, rad, blocks(firsts, 0.5, False), seconds)
    ret = swap(back.reshape(128, 8, 640))
    grads = leaf_b(u, y, got, occ, firsts_t, seconds, degree_table())
    updated = finish(ret.reshape(1024, 640), features, leaf_row, mats)
    return updated, grads


def solution(mesh):
    spread = P(AXES, None)
    across = P(None, AXES)
    return jax.shard_map(
        shards,
        mesh=mesh,
        in_specs=(spread, spread, spread, across, across) + (P(),) * 13,
        out_specs=(spread, across),
        check_vma=False,
    )
```
